512 devices in a mesh: req: 8 (over y), seq: 8 (over x, core), tp: 8 (over z).
Axes of the slice: x: 4, y: 8, z: 8, core: 2. Of those that a mesh axis runs over, the one named last changes fastest.
Arguments:
- tokens: bfloat16 [2048, 1024], P(('req', 'seq', 'tp')), may hold values from -3 to 3
- w_qkv: bfloat16 [1024, 3, 1024], P(None, None, 'tp'), may hold values from -0.1875 to 0.1875
- w_out: bfloat16 [1024, 1024], P('tp'), may hold values from -0.75 to 0.75
- variate_bias: float32 [2, 16], P(None, 'tp'), may hold values from -2 to 2
- attn_gain: float32 [1024], replicated, may hold values from 0.25 to 1.75
- ffn_gain: float32 [1024], replicated, may hold values from 0.25 to 1.75
- gate_up: bfloat16 [1024, 64, 128], P(None, ('seq', 'tp')), may hold values from -0.1875 to 0.1875
- w_down: bfloat16 [64, 64, 1024], P(('seq', 'tp')), may hold values from -0.09375 to 0.09375
- cache_keys: bfloat16 [1536, 256, 1024], P(('req', 'seq'), None, 'tp'), may hold values from -360 to 360
- cache_values: bfloat16 [1536, 256, 1024], P(('req', 'seq'), None, 'tp'), may hold values from -6 to 6
- cache_variate: int32 [1536, 256], P(('req', 'seq')), may hold values from 0 to 3
- new_variate: int32 [512, 4], P('req'), may hold values from 0 to 3
- piece_slot: int32 [512, 64], P('req'), may hold values from -1 to 191, as said below
- cache_len: int32 [512], P('req'), may hold values from 1 to 16384, as said below
Outputs:
- layer_out: bfloat16 [2048, 1024], P(('req', 'seq', 'tp'))
The draws below stay inside these ranges and needn't reach their ends.
Inputs may be any that keep to these rules, and one draw needn't show every extreme that they name: `cache_len`: in each aligned block of 64 requests exactly one request has the most cached positions. `piece_slot`: entry p of request r is the slot within its group that holds cache positions p * 256 to p * 256 + 255; it is -1 exactly when p * 256 >= cache_len[r]; no slot of a group holds two pieces; slots that hold no piece are never read.
All inputs are finite; a program needn't handle non-finite values.
Results may differ from the reference program's by a relative error of at most 0.022.
Values may be sent and summed in bfloat16 or wider, within the bound.
No kernel may reach another device: no remote copies, remote signals or barrier semaphores. Data moves between devices by JAX's collectives and lax.ppermute only.
A program may use at most 64 MiB of HBM per device.

```python
import math
import jax
import jax.numpy as jnp
from jax import lax

D = 1024
HEADS = 16
HD = 64
FF = 4096
UBLK = 64
STEPS = 4
PIECE = 256
VARIATES = 4
MAXP = 64
REQ_GRP = 64
GROUPS = 8
REQUESTS = 512
GROUP_SLOTS = 192
ALL_SLOTS = 1536
TOKROWS = 2048


def slot_table(key):

    def one_group(group_key):
        first_key, second_key, third_key = jax.random.split(group_key, 3)
        longest = jax.random.randint(first_key, (), 0, REQ_GRP)
        others = (GROUP_SLOTS - MAXP) // (REQ_GRP - 1)
        short_lengths = jax.random.randint(second_key, (REQ_GRP,), 1, others * PIECE + 1)
        request_ids = jnp.arange(REQ_GRP, dtype=jnp.int32)
        lengths = jnp.where(request_ids == longest, MAXP * PIECE, short_lengths).astype(jnp.int32)
        pieces = (lengths + PIECE - 1) // PIECE
        starts = jnp.cumsum(pieces) - pieces
        slot_order = jax.random.permutation(third_key, GROUP_SLOTS).astype(jnp.int32)
        long_start = jnp.sum(jnp.where(request_ids == longest, starts, 0))
        slot_ids = jnp.arange(GROUP_SLOTS, dtype=jnp.int32)
        displaced = jnp.sum(jnp.where(slot_ids == long_start, slot_order, 0))
        slot_order = jnp.where(slot_order == GROUP_SLOTS - 1, displaced, slot_order)
        slot_order = jnp.where(slot_ids == long_start, GROUP_SLOTS - 1, slot_order)
        piece_ids = jnp.arange(MAXP, dtype=jnp.int32)
        gather_at = jnp.minimum(starts[:, None] + piece_ids[None, :], GROUP_SLOTS - 1)
        table_rows = jnp.where(piece_ids[None, :] < pieces[:, None], slot_order[gather_at], -1)
        return (lengths, table_rows.astype(jnp.int32))
    group_keys = jax.random.split(jax.random.fold_in(key, 11), GROUPS)
    lengths, table_rows = jax.vmap(one_group)(group_keys)
    return (lengths.reshape(REQUESTS), table_rows.reshape(REQUESTS, MAXP))


def draw_cache_len(key, part):
    return slot_table(key)[0]


def draw_piece_slot(key, part):
    return slot_table(key)[1]


def draw_cache_keys(key, part):
    base = jnp.clip(jax.random.normal(key, (ALL_SLOTS, PIECE, D), jnp.float32), -6.0, 6.0)
    return base.astype(jnp.bfloat16)


def plant(drawn, key, low, top_value):
    longest = drawn.shape.index(max(drawn.shape))
    spots = []
    for shift in (0, 1):
        where = [jax.random.randint(jax.random.fold_in(key, axis), (), 0, length) for axis, length in enumerate(drawn.shape)]
        where[longest] = (where[longest] + shift) % drawn.shape[longest]
        spots.append(tuple(where))
    return drawn.at[spots[0]].set(low).at[spots[1]].set(top_value)


def level_of(stream_key, dims, shards, low, largest):
    level = 1.0
    for axis_at, blocks in shards:
        draws = jax.random.uniform(jax.random.fold_in(jax.random.fold_in(stream_key, 6), axis_at), (blocks,), jnp.float32, low / len(shards), largest / len(shards))
        level = level * jnp.repeat(jnp.exp(draws), dims[axis_at] // blocks).reshape((-1,) + (1,) * (len(dims) - 1 - axis_at))
    return level


def centred(stream_key, extent, scale, bound, cuts=(), held_as=jnp.bfloat16):
    drawn = scale * jax.random.normal(stream_key, extent, jnp.float32)
    if cuts:
        drawn = drawn * level_of(stream_key, extent, cuts, -0.22, 0.18)
    return jnp.clip(drawn, -bound, bound).astype(held_as)


def setup_inputs(seed: int = 0) -> dict:
    keys = jax.random.split(jax.random.key(seed), 15)
    return {
        "tokens": centred(keys[0], (TOKROWS, D), 0.5, 3.0, ((0, 512),)),
        "w_qkv": centred(keys[1], (D, 3, D), D ** -0.5, 0.1875, ((2, 8),)),
        "w_out": centred(keys[2], (D, D), HD ** -0.5, 0.75, ((0, 8),)),
        "variate_bias": jnp.clip(jax.random.uniform(keys[3], (2, HEADS), jnp.float32, -2.0, 2.0) * level_of(keys[3], (2, HEADS), ((1, 8),), -0.4, 0.0), -2.0, 2.0),
        "attn_gain": jnp.clip(1.0 + 0.15 * jax.random.normal(keys[4], (D,), jnp.float32), 0.25, 1.75),
        "ffn_gain": jnp.clip(1.0 + 0.15 * jax.random.normal(keys[5], (D,), jnp.float32), 0.25, 1.75),
        "gate_up": centred(keys[6], (D, FF // UBLK, 2 * UBLK), D ** -0.5, 0.1875, ((1, 64),)),
        "w_down": centred(keys[7], (FF // UBLK, UBLK, D), FF ** -0.5, 0.09375, ((0, 64),)),
        "cache_keys": draw_cache_keys(jax.random.fold_in(keys[14], 71), 0),
        "cache_values": centred(keys[9], (ALL_SLOTS, PIECE, D), 1.0, 6.0, ((0, 64), (2, 8))),
        "cache_variate": plant(jax.random.randint(keys[10], (ALL_SLOTS, PIECE), 0, VARIATES), jax.random.fold_in(keys[10], 1), 0, VARIATES - 1).astype(jnp.int32),
        "new_variate": plant(jax.random.randint(keys[11], (REQUESTS, STEPS), 0, VARIATES), jax.random.fold_in(keys[11], 1), 0, VARIATES - 1).astype(jnp.int32),
        "piece_slot": draw_piece_slot(jax.random.fold_in(keys[14], 71), 0),
        "cache_len": draw_cache_len(jax.random.fold_in(keys[14], 71), 0),
    }


EPSILON = 1e-05
MASKED_SCORE = -1e+30

def rms_scale(rows, gain):
    rows32 = rows.astype(jnp.float32)
    mean_sq = lax.optimization_barrier(jnp.mean(rows32 * rows32, axis=-1, keepdims=True))
    return (rows32 * lax.rsqrt(mean_sq + EPSILON) * gain.astype(jnp.float32)).astype(jnp.bfloat16)

def rotate(vectors, positions):
    half_size = vectors.shape[-1] // 2
    inv_freq = 10000.0 ** (-jnp.arange(half_size, dtype=jnp.float32) / half_size)
    angles = positions[:, None] * inv_freq[None, :]
    cosine = jnp.cos(angles)[:, None, :]
    sine_part = jnp.sin(angles)[:, None, :]
    earlier = vectors[..., :half_size]
    latter = vectors[..., half_size:]
    return jnp.concatenate([earlier * cosine - latter * sine_part, latter * cosine + earlier * sine_part], axis=-1)

def row_positions(lengths, step_count):
    offsets = jnp.arange(step_count, dtype=jnp.int32)
    return (lengths[:, None] + offsets[None, :]).reshape(-1).astype(jnp.float32)

def split_heads(projected, positions, head_size):
    row_count = projected.shape[0]
    parts = projected.reshape(row_count, 3, -1, head_size)
    queries = rotate(parts[:, 0], positions).astype(jnp.bfloat16)
    keys_new = rotate(parts[:, 1], positions).astype(jnp.bfloat16)
    values_new = parts[:, 2].astype(jnp.bfloat16)
    return (queries, keys_new, values_new)

def widen(array):
    return lax.optimization_barrier(array.astype(jnp.bfloat16)).astype(jnp.float32)

def reference(tokens, w_qkv, w_out, variate_bias, attn_gain, ffn_gain, gate_up, w_down, cache_keys, cache_values, cache_variate, new_variate, piece_slot, cache_len):
    score_scale = 1.0 / math.sqrt(HD)
    normed = rms_scale(tokens, attn_gain)
    projected = jnp.dot(normed, w_qkv.reshape(D, 3 * D), preferred_element_type=jnp.float32)
    queries, keys_new, values_new = split_heads(projected, row_positions(cache_len, STEPS), HD)
    shape_four = (REQUESTS, STEPS, HEADS, HD)
    group_ids = jnp.arange(REQUESTS, dtype=jnp.int32) // REQ_GRP
    same_bias = variate_bias[0][:, None, None]
    diff_bias = variate_bias[1][:, None, None]
    step_ids = jnp.arange(STEPS, dtype=jnp.int32)
    causal = step_ids[:, None] >= step_ids[None, :]

    def attend(inputs):
        query_rows, key_rows, value_rows, slot_row, length, variate, group_index = inputs
        slot_rows = (jnp.maximum(slot_row, 0) + group_index * GROUP_SLOTS).astype(jnp.int32)
        cache_k = jnp.take(cache_keys, slot_rows, axis=0).reshape(MAXP * PIECE, HEADS, HD).astype(jnp.float32)
        cache_v = jnp.take(cache_values, slot_rows, axis=0).reshape(MAXP * PIECE, HEADS, HD).astype(jnp.float32)
        cache_var = jnp.take(cache_variate, slot_rows, axis=0).reshape(MAXP * PIECE)
        is_valid = jnp.arange(MAXP * PIECE, dtype=jnp.int32) < length
        query32 = query_rows.astype(jnp.float32)
        same_cache = variate[:, None] == cache_var[None, :]
        cache_scores = jnp.einsum('thd,khd->htk', query32, cache_k) * score_scale
        cache_scores = cache_scores + jnp.where(same_cache[None], same_bias, diff_bias)
        cache_scores = jnp.where(is_valid[None, None, :], cache_scores, MASKED_SCORE)
        same_new = variate[:, None] == variate[None, :]
        new_scores = jnp.einsum('thd,uhd->htu', query32, key_rows.astype(jnp.float32)) * score_scale
        new_scores = new_scores + jnp.where(same_new[None], same_bias, diff_bias)
        new_scores = jnp.where(causal[None], new_scores, MASKED_SCORE)
        row_top = jnp.maximum(lax.optimization_barrier(jnp.max(cache_scores, axis=2)), lax.optimization_barrier(jnp.max(new_scores, axis=2)))
        cache_weights = jnp.where(is_valid[None, None, :], jnp.exp(cache_scores - row_top[..., None]), 0.0)
        new_weights = jnp.where(causal[None], jnp.exp(new_scores - row_top[..., None]), 0.0)
        row_total = lax.optimization_barrier(jnp.sum(cache_weights, axis=2)) + lax.optimization_barrier(jnp.sum(new_weights, axis=2))
        mixed_out = jnp.einsum('htk,khd->htd', widen(cache_weights), cache_v)
        mixed_out = mixed_out + jnp.einsum('htu,uhd->htd', widen(new_weights), value_rows.astype(jnp.float32))
        attended = mixed_out / row_total[..., None]
        return jnp.transpose(attended, (1, 0, 2)).reshape(STEPS, D).astype(jnp.bfloat16)
    attended = lax.map(attend, (queries.reshape(shape_four), keys_new.reshape(shape_four), values_new.reshape(shape_four), piece_slot, cache_len, new_variate, group_ids))
    attended = attended.reshape(TOKROWS, D)
    mid = tokens.astype(jnp.float32) + jnp.dot(attended, w_out, preferred_element_type=jnp.float32)
    normed_mid = rms_scale(mid, ffn_gain)
    blocks = FF // UBLK
    expanded = jnp.dot(normed_mid, gate_up.reshape(D, blocks * 2 * UBLK), preferred_element_type=jnp.float32).reshape(TOKROWS, blocks, 2 * UBLK)
    hidden = (jax.nn.silu(expanded[:, :, :UBLK]) * expanded[:, :, UBLK:]).astype(jnp.bfloat16).reshape(TOKROWS, FF)
    ffn_rows = jnp.dot(hidden, w_down.reshape(FF, D), preferred_element_type=jnp.float32)
    return (mid + ffn_rows).astype(jnp.bfloat16)
```

```python
import math

import jax
import jax.numpy as jnp
import numpy as np
from jax import lax
from jax.experimental import pallas as pl
from jax.experimental.pallas import tpu as pltpu
from jax.sharding import PartitionSpec as P

HD = 64
EPSILON = 1e-05
MASKED_SCORE = -1e30
FAR = -1e38
LANES = 128
INTERPRET = False


def exchange(pieces, axes):
    return lax.all_to_all(pieces, axes, 0, 0, tiled=True)


def copies(block, axes):
    return jnp.broadcast_to(block[None], (lax.axis_size(axes), *block.shape))


def swapped(blocks, partner):
    return lax.ppermute(blocks, "seq", list(enumerate(partner)))


def in_vmem(count):
    return [pl.BlockSpec(memory_space=pltpu.VMEM)] * count


def in_smem(count):
    return [pl.BlockSpec(memory_space=pltpu.SMEM)] * count


def stay_in_hbm(array):
    return array if INTERPRET else pltpu.with_memory_space_constraint(array, pltpu.HBM)


def kernel_call(body, out_shape, in_specs, name, moved, loads=(), small=(), scratch=()):
    many = isinstance(out_shape, (list, tuple))
    outs = len(out_shape) if many else 1
    held = [pltpu.VMEM(a.shape, a.dtype) for a in loads] + [
        pltpu.SMEM(a.shape, a.dtype) for a in small
    ]
    count, plain = len(held), len(in_specs)

    def run(*refs):
        ins, refs = refs[:plain], refs[plain:]
        sources, refs = refs[:count], refs[count:]
        results, refs = refs[:outs], refs[outs:]
        buffers, refs = refs[:count], refs[count:]
        sems, rest = refs[:count], refs[count:]
        moves = [pltpu.make_async_copy(*each) for each in zip(sources, buffers, sems)]
        for move in moves:
            move.start()

        def arrive(*which):
            for i in which or range(count):
                moves[i].wait()

        body(arrive, *ins, *buffers, *results, *rest)

    call = pl.pallas_call(
        run,
        out_shape=out_shape,
        in_specs=list(in_specs) + [pl.BlockSpec(memory_space=pltpu.HBM)] * count,
        out_specs=in_vmem(outs) if many else in_vmem(1)[0],
        scratch_shapes=held + [pltpu.SemaphoreType.DMA(())] * count + list(scratch),
        name=name,
        interpret=INTERPRET,
        compiler_params=pltpu.CompilerParams(vmem_limit_bytes=16 << 20),
        cost_estimate=pl.CostEstimate(flops=300 * moved, bytes_accessed=moved, transcendentals=0),
    )
    return lambda *ins: call(*ins, *[stay_in_hbm(a) for a in (*loads, *small)])


def iota(shape, dim):
    return lax.broadcasted_iota(jnp.int32, shape, dim)


def matmul(a, b):
    return jnp.dot(a, b, preferred_element_type=jnp.float32)


def matmul_t(a, b):
    return lax.dot_general(a, b, (((1,), (1,)), ((), ())), preferred_element_type=jnp.float32)


def scaled_rows(rows, gain):
    mean_sq = jnp.mean(rows * rows, axis=-1, keepdims=True)
    return (rows * lax.rsqrt(mean_sq + EPSILON) * gain).astype(jnp.bfloat16)


def stacked(ref):
    return jnp.concatenate([ref[i].astype(jnp.float32) for i in range(ref.shape[0])], axis=0)


def pack_body(arrive, gate_ref, down_ref, out_ref):
    arrive()
    depth = gate_ref.shape[0]
    units = down_ref.shape[0]
    out_ref[0, :depth] = gate_ref[...]
    for c in range(down_ref.shape[1] // LANES):
        at = depth + units * c
        out_ref[0, at : at + units] = down_ref[:, LANES * c : LANES * (c + 1)]


def join_body(arrive, first_ref, second_ref, after_ref, out_ref):
    count = first_ref.shape[0]
    out_ref[:count] = first_ref[...]
    out_ref[count:] = second_ref[...]


def joined(first, second, after):
    return kernel_call(
        join_body,
        jax.ShapeDtypeStruct((2 * first.shape[0], *first.shape[1:]), first.dtype),
        in_vmem(2) + [pl.BlockSpec(memory_space=pl.ANY)],
        "join",
        moved=4 << 20,
    )(first, second, after)


def project_body(arrive, token_ref, cos_ref, sin_ref, gain_ref, w_ref, q_ref, k_ref, v_ref):
    arrive(0)
    normed = scaled_rows(stacked(token_ref), gain_ref[...])
    cosine, sine = stacked(cos_ref), stacked(sin_ref)
    first_half = iota(cosine.shape, 1) % HD < HD // 2

    def rotate(part):
        partner = jnp.where(
            first_half,
            pltpu.roll(part, LANES - HD // 2, 1),
            pltpu.roll(part, HD // 2, 1),
        )
        return (part * cosine + partner * sine).astype(jnp.bfloat16)

    arrive(1)
    queries = rotate(matmul(normed, w_ref[0]))
    for i in range(q_ref.shape[0]):
        q_ref[i] = queries
    k_ref[...] = rotate(matmul(normed, w_ref[1]))
    v_ref[...] = matmul(normed, w_ref[2]).astype(jnp.bfloat16)


def fresh_part(steps, scale, packed, q_ref, k_ref, v_ref, bias_ref, out_ref, lse_ref):
    queries = q_ref[0]
    rows = queries.shape[0]
    packed = jnp.concatenate(
        [jnp.broadcast_to(packed[i : i + 1, :rows], (steps, rows)) for i in range(packed.shape[0])],
        axis=0,
    )
    low_lanes = iota((rows, LANES), 1) < HD
    split = [
        jnp.where(low_lanes, queries, jnp.zeros_like(queries)),
        jnp.where(low_lanes, jnp.zeros_like(queries), queries),
    ]
    row_id, col_id = iota((rows, rows), 0), iota((rows, rows), 1)
    allowed = (row_id // steps == col_id // steps) & (row_id % steps >= col_id % steps)
    same = (packed >> (2 * (row_id % steps))) & 3 == (packed >> (2 * (col_id % steps))) & 3
    outs, lses = [], []
    for head in range(2):
        scores = matmul_t(split[head], k_ref[...]) * scale
        scores = scores + jnp.where(same, bias_ref[0, head], bias_ref[1, head])
        scores = jnp.where(allowed, scores, MASKED_SCORE)
        top = jnp.max(scores, axis=1, keepdims=True)
        weights = jnp.where(allowed, jnp.exp(scores - top), 0.0)
        total = jnp.sum(weights, axis=1, keepdims=True)
        outs.append(matmul(weights.astype(jnp.bfloat16), v_ref[...]) / total)
        lses.append(top + jnp.log(total))
    out_ref[...] = jnp.where(low_lanes, outs[0], outs[1])
    lse_ref[...] = jnp.where(low_lanes, lses[0], lses[1])


def prepare_body(
    steps,
    slots,
    scale,
    arrive,
    seq_ref,
    q_ref,
    k_ref,
    v_ref,
    slot_ref,
    len_ref,
    variate_ref,
    cached_variate_ref,
    bias_ref,
    pick_ref,
    place_ref,
    same_ref,
    bias_mask_ref,
    fresh_ref,
    fresh_lse_ref,
    packed_ref,
):
    requests, pieces = slot_ref.shape
    piece_len = cached_variate_ref.shape[1]
    group = 2 * steps
    rows = slots * group
    arrive()
    table = slot_ref[...]
    packed_row = variate_ref[0:1, :]
    for t in range(1, steps):
        packed_row = packed_row + (variate_ref[t : t + 1, :] << (2 * t))
    columns = jnp.where(iota((8, requests), 0) == 0, packed_row, len_ref[...])
    columns = jnp.transpose(columns.astype(jnp.float32)).astype(jnp.int32)
    packed_variate, length = columns[:, 0:1], columns[:, 1:2]
    packed_ref[...] = jnp.broadcast_to(packed_variate, (requests, LANES))
    own = requests // (requests * steps // q_ref.shape[1])
    packed = packed_ref[pl.ds(pl.multiple_of(seq_ref[0] * own, own), own), :]
    fresh_part(steps, scale, packed, q_ref, k_ref, v_ref, bias_ref, fresh_ref, fresh_lse_ref)

    live = jnp.clip(length - piece_len * iota((requests, pieces), 1), 0, piece_len)
    code = (iota((requests, pieces), 0) << 17) + (packed_variate << 9) + live
    code = code.astype(jnp.float32)
    base = seq_ref[0] * slots
    found = []
    for s in range(slots):
        hit = jnp.where(table == base + s, code, -1.0)
        hit = jnp.max(jnp.max(hit, axis=0, keepdims=True), axis=1, keepdims=True)
        found.append(jnp.broadcast_to(hit, (group, LANES)))
    found = jnp.concatenate(found, axis=0)
    found_lane = jnp.transpose(found)[0:1, :].astype(jnp.int32)
    found = found[:, 0:1].astype(jnp.int32)
    owned = found >= 0
    owner = jnp.where(owned, found >> 17, -1)
    owner_lane = jnp.where(found_lane >= 0, found_lane >> 17, -1)
    row_in = iota((rows, 1), 0) % group
    step_row = row_in % steps
    lane_in = iota((1, rows), 1) % group

    wide = (rows, requests * steps)
    pick_ref[...] = jnp.where(
        iota(wide, 1) == jnp.where(owned, owner * steps + step_row, -1), 1.0, 0.0
    ).astype(jnp.bfloat16)
    tall = (requests * steps, rows)
    place_ref[...] = jnp.where(
        iota(tall, 0) == jnp.where(owner_lane >= 0, owner_lane * steps + lane_in % steps, -1),
        1.0,
        0.0,
    ).astype(jnp.bfloat16)
    same_ref[...] = jnp.where((owner == owner_lane) & (row_in == lane_in), 0.0, FAR)

    limit = jnp.where(owned, found & 511, 0)
    variate = (found >> (9 + 2 * step_row)) & 3
    first_head = row_in < steps
    same_bias = jnp.where(first_head, bias_ref[0, 0], bias_ref[0, 1])
    other_bias = jnp.where(first_head, bias_ref[1, 0], bias_ref[1, 1])
    cached = jnp.concatenate(
        [
            jnp.broadcast_to(cached_variate_ref[s : s + 1, :], (group, piece_len))
            for s in range(slots)
        ],
        axis=0,
    )
    biases = jnp.where(variate == cached, same_bias, other_bias)
    bias_mask_ref[...] = jnp.where(iota((rows, piece_len), 1) < limit, biases, MASKED_SCORE)


def two_terms(value):
    high = value.astype(jnp.bfloat16)
    return high, (value - high.astype(jnp.float32)).astype(jnp.bfloat16)


def cache_body(
    steps, scale, arrive, q_ref, pick_ref, place_ref, same_ref, bias_mask_ref, k_ref, v_ref, out_ref
):
    slots = k_ref.shape[0]
    group = 2 * steps
    rows = slots * group
    devices = out_ref.shape[0]
    span = out_ref.shape[1] // 2
    all_queries = jnp.concatenate([q_ref[i] for i in range(devices)], axis=0)
    picked = matmul(pick_ref[...], all_queries)
    row_head = iota((rows, LANES), 0) % group // steps
    head_match = row_head == iota((rows, LANES), 1) // HD
    picked = jnp.where(head_match, picked, 0.0)
    scores = jnp.concatenate(
        [
            matmul_t(picked[group * s : group * (s + 1)].astype(jnp.bfloat16), k_ref[s])
            for s in range(slots)
        ],
        axis=0,
    )
    bias_mask = bias_mask_ref[...]
    live = bias_mask > 0.5 * MASKED_SCORE
    scores = jnp.where(live, scores * scale + bias_mask, MASKED_SCORE)
    slot_top = jnp.max(scores, axis=1, keepdims=True)
    top_lane = jnp.transpose(jnp.broadcast_to(slot_top, (rows, LANES)))[0:1, :]
    row_top = jnp.max(top_lane + same_ref[...], axis=1, keepdims=True)
    weights = jnp.where(live, jnp.exp(scores - row_top), 0.0)
    total = jnp.sum(weights, axis=1, keepdims=True)
    arrive(0)
    mixed = jnp.concatenate(
        [
            matmul(weights[group * s : group * (s + 1)].astype(jnp.bfloat16), v_ref[s])
            for s in range(slots)
        ],
        axis=0,
    )
    both = jnp.concatenate(
        [jnp.where(head_match, mixed, 0.0), jnp.where(head_match, total, 0.0)], axis=1
    )
    high, low = two_terms(both)
    place = place_ref[...]
    summed = matmul(place, high) + matmul(place, low)
    out_sum, total_sum = summed[:, :LANES], summed[:, LANES:]
    lane_head = iota((1, rows), 1) % group // steps
    placed = place.astype(jnp.float32) > 0.5
    tops = [
        jnp.max(jnp.where(placed & (lane_head == h), top_lane, MASKED_SCORE), axis=1, keepdims=True)
        for h in range(2)
    ]
    low_lanes = iota(out_sum.shape, 1) < HD
    top = jnp.where(low_lanes, tops[0], tops[1])
    some = total_sum > 0.0
    safe_total = jnp.where(some, total_sum, 1.0)
    averaged = jnp.where(some, out_sum / safe_total, 0.0).astype(jnp.bfloat16)
    lse = jnp.where(some, top + jnp.log(safe_total), MASKED_SCORE)
    lse_high = lse.astype(jnp.bfloat16).astype(jnp.float32)
    rest = lse - lse_high
    lse_mid = rest.astype(jnp.bfloat16).astype(jnp.float32)
    place_in = iota(out_sum.shape, 1) % HD
    coded = jnp.where(
        place_in == 0,
        lse_high,
        jnp.where(place_in == 1, lse_mid, jnp.where(place_in == 2, rest - lse_mid, 0.0)),
    ).astype(jnp.bfloat16)
    for d in range(devices):
        out_ref[d, :span] = averaged[span * d : span * (d + 1)]
        out_ref[d, span:] = coded[span * d : span * (d + 1)]


def finish_body(arrive, part_ref, fresh_ref, fresh_lse_ref, w_ref, out_ref):
    devices = part_ref.shape[0]
    span = part_ref.shape[1] // 2
    source, lane = iota((LANES, LANES), 0), iota((LANES, LANES), 1)
    decode = jnp.where((source // HD == lane // HD) & (source % HD < 3), 1.0, 0.0)
    decode = decode.astype(jnp.bfloat16)
    lses = [matmul(part_ref[d, span:], decode) for d in range(devices)]
    top = fresh_lse_ref[...]
    for lse in lses:
        top = jnp.maximum(top, lse)
    weight = jnp.exp(fresh_lse_ref[...] - top)
    total = weight
    mixed = weight * fresh_ref[...]
    for d in range(devices):
        weight = jnp.exp(lses[d] - top)
        total = total + weight
        mixed = mixed + weight * part_ref[d, :span].astype(jnp.float32)
    attended = (mixed / total).astype(jnp.bfloat16)
    arrive()
    partial = matmul(attended, w_ref[...]).astype(jnp.bfloat16)
    for d in range(out_ref.shape[0]):
        out_ref[d] = partial


def feed(normed, w_ref):
    rows, width = normed.shape
    blocks = [w_ref.at[i] for i in range(w_ref.shape[0])]
    low_lanes = iota((rows, LANES), 1) < HD
    halves = []
    for s, block in enumerate(blocks):
        expanded = matmul(normed, block[:width])
        gate = expanded / (1.0 + jnp.exp(-expanded))
        part = gate * pltpu.roll(expanded, HD, 1)
        if s % 2 == 0:
            halves.append(part)
        else:
            halves[-1] = jnp.where(low_lanes, halves[-1], pltpu.roll(part, HD, 1))
    hidden = jnp.concatenate(halves, axis=1).astype(jnp.bfloat16)
    parts = []
    for c in range(width // LANES):
        at = width + HD * c
        weights = jnp.concatenate([block[at : at + HD] for block in blocks], axis=0)
        parts.append(matmul(hidden, weights))
    return parts


def feed_own_body(arrive, part_ref, token_ref, w_ref, gain_ref, out_ref, normed_ref, mid_ref):
    mid = part_ref[0].astype(jnp.float32)
    for d in range(1, part_ref.shape[0]):
        mid = mid + part_ref[d].astype(jnp.float32)
    mid = mid + stacked(token_ref)
    own = mid_ref.shape[1]
    for d in range(mid_ref.shape[0]):
        mid_ref[d] = mid[own * d : own * (d + 1)]
    arrive()
    normed = scaled_rows(mid, gain_ref[...])
    normed_ref[...] = normed
    for c, part in enumerate(feed(normed, w_ref)):
        out_ref[:, LANES * c : LANES * (c + 1)] = part


def feed_near_body(arrive, normed_ref, w_ref, part_ref, out_ref):
    own = out_ref.shape[1]
    for c, part in enumerate(feed(normed_ref[...], w_ref)):
        lanes = slice(LANES * c, LANES * (c + 1))
        part = part + part_ref[:, lanes]
        for d in range(out_ref.shape[0]):
            out_ref[d, :, lanes] = part[own * d : own * (d + 1)].astype(jnp.bfloat16)


def last_body(arrive, index_ref, part_ref, mid_ref, out_ref):
    total = mid_ref[index_ref[0]]
    summed = part_ref[0].astype(jnp.float32)
    for d in range(1, part_ref.shape[0]):
        summed = summed + part_ref[d].astype(jnp.float32)
    out_ref[...] = (total + summed).astype(jnp.bfloat16)


def rotation_tables(lengths, steps):
    half = HD // 2
    lane = np.arange(LANES)
    inv_freq = (10000.0 ** (-(lane % half) / half)).astype(np.float32)
    sign = np.where(lane % HD < half, -1.0, 1.0).astype(np.float32)
    offsets = jnp.arange(steps, dtype=jnp.int32)
    positions = (lengths[:, None, None] + offsets[None, :, None]).astype(jnp.float32)
    angles = positions * inv_freq
    return jnp.cos(angles), jnp.sin(angles) * sign


def on_device(
    tokens,
    w_qkv,
    w_out,
    variate_bias,
    attn_gain,
    ffn_gain,
    gate_up,
    w_down,
    cache_keys,
    cache_values,
    cache_variate,
    new_variate,
    piece_slot,
    cache_len,
):
    row_count, width = tokens.shape
    requests, steps = new_variate.shape
    slots, piece_len, lanes = cache_keys.shape
    seqs, tps = lax.axis_size("seq"), lax.axis_size("tp")
    rows = row_count * tps
    own_requests = rows // steps
    scale = 1.0 / math.sqrt(HD)
    bf16, f32 = jnp.bfloat16, jnp.float32
    shape = jax.ShapeDtypeStruct
    seq_at = lax.axis_index("seq")
    tp_at = lax.axis_index("tp").astype(jnp.int32).reshape(1)

    row_tokens = exchange(copies(tokens, "tp"), "tp")

    blocks, units = w_down.shape[:2]
    ffn_weights = kernel_call(
        pack_body,
        shape((1, width + units * width // lanes, lanes), bf16),
        [],
        "pack",
        moved=1 << 20,
        loads=[gate_up.reshape(width, lanes), w_down.reshape(units, width)],
    )()
    ffn_next = swapped(ffn_weights, [2, 3, 0, 1, 6, 7, 4, 5])

    own_len = lax.dynamic_slice_in_dim(cache_len, seq_at * own_requests, own_requests, 0)
    cosine, sine = rotation_tables(own_len, steps)
    queries, keys_new, values_new = kernel_call(
        project_body,
        [shape((seqs, rows, lanes), bf16), shape((rows, lanes), bf16), shape((rows, lanes), bf16)],
        in_vmem(3),
        "project",
        moved=1 << 20,
        loads=[attn_gain[None, :], w_qkv.transpose(1, 0, 2)],
    )(row_tokens, cosine, sine)
    all_queries = exchange(queries, "seq")

    slot_rows = 2 * steps * slots
    pick, place, same, bias_mask, fresh, fresh_lse = kernel_call(
        lambda *refs: prepare_body(steps, slots, scale, *refs),
        [
            shape((slot_rows, requests * steps), bf16),
            shape((requests * steps, slot_rows), bf16),
            shape((slot_rows, slot_rows), f32),
            shape((slot_rows, piece_len), f32),
            shape((rows, lanes), f32),
            shape((rows, lanes), f32),
        ],
        in_smem(1) + in_vmem(3),
        "prepare",
        moved=1 << 20,
        loads=[piece_slot, cache_len[None, :], new_variate.T, cache_variate],
        small=[variate_bias],
        scratch=[pltpu.VMEM((requests, lanes), jnp.int32)],
    )(seq_at.astype(jnp.int32).reshape(1), queries, keys_new, values_new)

    partial = kernel_call(
        lambda *refs: cache_body(steps, scale, *refs),
        shape((seqs, 2 * rows, lanes), bf16),
        in_vmem(6),
        "cache",
        moved=4 << 20,
        loads=[cache_values],
    )(all_queries, pick, place, same, bias_mask, cache_keys)
    ffn_weights = joined(ffn_weights, ffn_next, partial)
    partial = exchange(partial, "seq")

    ffn_far = swapped(ffn_weights, [6, 7, 4, 5, 2, 3, 0, 1])
    mid_parts = kernel_call(
        finish_body,
        shape((tps, rows, width), bf16),
        in_vmem(3),
        "finish",
        moved=30 << 20,
        loads=[w_out],
    )(partial, fresh, fresh_lse)
    ffn_weights = joined(ffn_weights, ffn_far, mid_parts)
    mid_parts = exchange(mid_parts, "tp")
    ffn_near = swapped(ffn_weights, [1, 0, 3, 2, 5, 4, 7, 6])
    ffn_sum, normed, mid = kernel_call(
        feed_own_body,
        [
            shape((rows, width), f32),
            shape((rows, width), bf16),
            shape((tps, row_count, width), f32),
        ],
        in_vmem(3),
        "feed_own",
        moved=30 << 20,
        loads=[ffn_gain[None, :]],
    )(mid_parts, row_tokens, ffn_weights)
    ffn_parts = kernel_call(
        feed_near_body,
        shape((tps, row_count, width), bf16),
        in_vmem(3),
        "feed_near",
        moved=4 << 20,
    )(normed, ffn_near, ffn_sum)
    ffn_parts = exchange(ffn_parts, "tp")
    return kernel_call(
        last_body, shape((row_count, width), bf16), in_smem(1) + in_vmem(2), "last", moved=1 << 17
    )(tp_at, ffn_parts, mid)


def solution(mesh):
    in_specs = (
        P(("req", "seq", "tp"), None),
        P(None, None, "tp"),
        P("tp", None),
        P(None, "tp"),
        P(),
        P(),
        P(None, ("seq", "tp"), None),
        P(("seq", "tp"), None, None),
        P(("req", "seq"), None, "tp"),
        P(("req", "seq"), None, "tp"),
        P(("req", "seq"), None),
        P("req", None),
        P("req", None),
        P("req"),
    )
    out_specs = P(("req", "seq", "tp"), None)
    return jax.shard_map(
        on_device, mesh=mesh, in_specs=in_specs, out_specs=out_specs, check_vma=False
    )
```

```python
import math

import jax
import jax.numpy as jnp
import numpy as np
from jax import lax
from jax.experimental import pallas as pl
from jax.experimental.pallas import tpu as pltpu
from jax.sharding import PartitionSpec as P

HD = 64
EPSILON = 1e-05
MASKED_SCORE = -1e30
FAR = -1e38
LANES = 128
INTERPRET = False


def exchange(pieces, axes):
    return lax.all_to_all(pieces, axes, 0, 0, tiled=True)


def swapped(blocks, partner):
    return lax.ppermute(blocks, "seq", list(enumerate(partner)))


def in_vmem(count):
    return [pl.BlockSpec(memory_space=pltpu.VMEM)] * count


def in_smem(count):
    return [pl.BlockSpec(memory_space=pltpu.SMEM)] * count


def stay_in_hbm(array):
    return array if INTERPRET else pltpu.with_memory_space_constraint(array, pltpu.HBM)


class Part:
    def __init__(self, array, start=0, size=None):
        self.array, self.start = array, start
        self.shape = (array.shape[0] if size is None else size, *array.shape[1:])
        self.dtype = array.dtype

    def of(self, ref):
        return ref if self.shape == ref.shape else ref.at[pl.ds(self.start, self.shape[0])]


def kernel_call(
    body, out_shape, in_specs, name, moved, loads=(), small=(), carried=(), scratch=()
):
    loads, small, carried = (
        [a if isinstance(a, Part) else Part(a) for a in arrays] for arrays in (loads, small, carried)
    )
    many = isinstance(out_shape, (list, tuple))
    shapes = list(out_shape) if many else [out_shape]
    outs = len(shapes)
    shapes = shapes + [jax.ShapeDtypeStruct(a.shape, a.dtype) for a in carried]
    held = [pltpu.VMEM(a.shape, a.dtype) for a in loads] + [
        pltpu.SMEM(a.shape, a.dtype) for a in small
    ]
    count, more, plain = len(held), len(carried), len(in_specs)

    def run(*refs):
        ins, refs = refs[:plain], refs[plain:]
        sources, refs = refs[: count + more], refs[count + more :]
        results, refs = refs[: outs + more], refs[outs + more :]
        buffers, refs = refs[:count], refs[count:]
        sems, rest = refs[: count + more], refs[count + more :]
        targets = [*buffers, *results[outs:]]
        sources = [a.of(ref) for a, ref in zip((*loads, *small, *carried), sources)]
        moves = [pltpu.make_async_copy(*each) for each in zip(sources, targets, sems)]
        for move in moves:
            move.start()

        def arrive(*which):
            for i in which or range(count):
                moves[i].wait()

        body(arrive, *ins, *buffers, *results[:outs], *rest)
        for move in moves[count:]:
            move.wait()

    call = pl.pallas_call(
        run,
        out_shape=shapes if many or more else shapes[0],
        in_specs=list(in_specs) + [pl.BlockSpec(memory_space=pltpu.HBM)] * (count + more),
        out_specs=in_vmem(outs + more) if many or more else in_vmem(1)[0],
        scratch_shapes=held + [pltpu.SemaphoreType.DMA(())] * (count + more) + list(scratch),
        name=name,
        interpret=INTERPRET,
        compiler_params=pltpu.CompilerParams(vmem_limit_bytes=8 << 20),
        cost_estimate=pl.CostEstimate(flops=300 * moved, bytes_accessed=moved, transcendentals=0),
    )
    return lambda *ins: call(*ins, *[stay_in_hbm(a.array) for a in (*loads, *small, *carried)])


def iota(shape, dim):
    return lax.broadcasted_iota(jnp.int32, shape, dim)


def matmul(a, b):
    return jnp.dot(a, b, preferred_element_type=jnp.float32)


def matmul_t(a, b):
    return lax.dot_general(a, b, (((1,), (1,)), ((), ())), preferred_element_type=jnp.float32)


def scaled_rows(rows, gain):
    mean_sq = jnp.mean(rows * rows, axis=-1, keepdims=True)
    return (rows * lax.rsqrt(mean_sq + EPSILON) * gain).astype(jnp.bfloat16)


def stacked(ref):
    return jnp.concatenate([ref[i].astype(jnp.float32) for i in range(ref.shape[0])], axis=0)


def pack_body(arrive, gate_ref, down_ref, out_ref):
    arrive()
    depth = gate_ref.shape[0]
    units = down_ref.shape[0]
    out_ref[0, :depth] = gate_ref[...]
    for c in range(down_ref.shape[1] // LANES):
        at = depth + units * c
        out_ref[0, at : at + units] = down_ref[:, LANES * c : LANES * (c + 1)]


def join_body(_, first_ref, second_ref, after_ref, out_ref, sem):
    count = first_ref.shape[0]
    move = pltpu.make_async_copy(second_ref, out_ref.at[pl.ds(count, count)], sem)
    move.start()
    out_ref[:count] = first_ref[...]
    move.wait()


def joined(first, second, after, carried=()):
    return kernel_call(
        join_body,
        jax.ShapeDtypeStruct((2 * first.shape[0], *first.shape[1:]), first.dtype),
        in_vmem(1) + [pl.BlockSpec(memory_space=pltpu.HBM), pl.BlockSpec(memory_space=pl.ANY)],
        "join",
        moved=4 << 20,
        carried=carried,
        scratch=[pltpu.SemaphoreType.DMA(())],
    )(first, stay_in_hbm(second), after)


def project_body(arrive, token_ref, cos_ref, sin_ref, gain_ref, w_ref, q_ref, k_ref, v_ref):
    normed = scaled_rows(stacked(token_ref), gain_ref[...])
    cosine, sine = stacked(cos_ref), stacked(sin_ref)
    first_half = iota(cosine.shape, 1) % HD < HD // 2

    def rotate(part):
        partner = jnp.where(
            first_half,
            pltpu.roll(part, LANES - HD // 2, 1),
            pltpu.roll(part, HD // 2, 1),
        )
        return (part * cosine + partner * sine).astype(jnp.bfloat16)

    queries = rotate(matmul(normed, w_ref[0]))
    for i in range(q_ref.shape[0]):
        q_ref[i] = queries
    k_ref[...] = rotate(matmul(normed, w_ref[1]))
    v_ref[...] = matmul(normed, w_ref[2]).astype(jnp.bfloat16)


def fresh_part(steps, scale, packed, q_ref, k_ref, v_ref, bias_ref, out_ref, lse_ref):
    queries = q_ref[0]
    rows = queries.shape[0]
    packed = jnp.concatenate(
        [jnp.broadcast_to(packed[i : i + 1, :rows], (steps, rows)) for i in range(packed.shape[0])],
        axis=0,
    )
    low_lanes = iota((rows, LANES), 1) < HD
    split = [
        jnp.where(low_lanes, queries, jnp.zeros_like(queries)),
        jnp.where(low_lanes, jnp.zeros_like(queries), queries),
    ]
    row_id, col_id = iota((rows, rows), 0), iota((rows, rows), 1)
    allowed = (row_id // steps == col_id // steps) & (row_id % steps >= col_id % steps)
    same = (packed >> (2 * (row_id % steps))) & 3 == (packed >> (2 * (col_id % steps))) & 3
    outs, lses = [], []
    for head in range(2):
        scores = matmul_t(split[head], k_ref[...]) * scale
        scores = scores + jnp.where(same, bias_ref[0, head], bias_ref[1, head])
        scores = jnp.where(allowed, scores, MASKED_SCORE)
        top = jnp.max(scores, axis=1, keepdims=True)
        weights = jnp.where(allowed, jnp.exp(scores - top), 0.0)
        total = jnp.sum(weights, axis=1, keepdims=True)
        outs.append(matmul(weights.astype(jnp.bfloat16), v_ref[...]) / total)
        lses.append(top + jnp.log(total))
    out_ref[...] = jnp.where(low_lanes, outs[0], outs[1])
    lse_ref[...] = jnp.where(low_lanes, lses[0], lses[1])


def prepare_body(
    steps,
    slots,
    scale,
    arrive,
    seq_ref,
    q_ref,
    k_ref,
    v_ref,
    slot_ref,
    len_ref,
    variate_ref,
    cached_variate_ref,
    bias_ref,
    pick_ref,
    place_ref,
    same_ref,
    bias_mask_ref,
    fresh_ref,
    fresh_lse_ref,
    packed_ref,
):
    requests, pieces = slot_ref.shape
    piece_len = cached_variate_ref.shape[1]
    group = 2 * steps
    rows = slots * group
    arrive()
    table = slot_ref[...]
    packed_row = variate_ref[0:1, :]
    for t in range(1, steps):
        packed_row = packed_row + (variate_ref[t : t + 1, :] << (2 * t))
    columns = jnp.where(iota((8, requests), 0) == 0, packed_row, len_ref[...])
    columns = jnp.transpose(columns.astype(jnp.float32)).astype(jnp.int32)
    packed_variate, length = columns[:, 0:1], columns[:, 1:2]
    packed_ref[...] = jnp.broadcast_to(packed_variate, (requests, LANES))
    own = requests // (requests * steps // q_ref.shape[1])
    packed = packed_ref[pl.ds(pl.multiple_of(seq_ref[0] * own, own), own), :]
    fresh_part(steps, scale, packed, q_ref, k_ref, v_ref, bias_ref, fresh_ref, fresh_lse_ref)

    live = jnp.clip(length - piece_len * iota((requests, pieces), 1), 0, piece_len)
    code = (iota((requests, pieces), 0) << 17) + (packed_variate << 9) + live
    code = code.astype(jnp.float32)
    base = seq_ref[0] * slots
    found = []
    for s in range(slots):
        hit = jnp.where(table == base + s, code, -1.0)
        hit = jnp.max(jnp.max(hit, axis=0, keepdims=True), axis=1, keepdims=True)
        found.append(jnp.broadcast_to(hit, (group, LANES)))
    found = jnp.concatenate(found, axis=0)
    found_lane = jnp.transpose(found)[0:1, :].astype(jnp.int32)
    found = found[:, 0:1].astype(jnp.int32)
    owned = found >= 0
    owner = jnp.where(owned, found >> 17, -1)
    owner_lane = jnp.where(found_lane >= 0, found_lane >> 17, -1)
    row_in = iota((rows, 1), 0) % group
    step_row = row_in % steps
    lane_in = iota((1, rows), 1) % group

    wide = (rows, requests * steps)
    pick_ref[...] = jnp.where(
        iota(wide, 1) == jnp.where(owned, owner * steps + step_row, -1), 1.0, 0.0
    ).astype(jnp.bfloat16)
    tall = (requests * steps, rows)
    place_ref[...] = jnp.where(
        iota(tall, 0) == jnp.where(owner_lane >= 0, owner_lane * steps + lane_in % steps, -1),
        1.0,
        0.0,
    ).astype(jnp.bfloat16)
    same_ref[...] = jnp.where((owner == owner_lane) & (row_in == lane_in), 0.0, FAR)

    limit = jnp.where(owned, found & 511, 0)
    variate = (found >> (9 + 2 * step_row)) & 3
    first_head = row_in < steps
    same_bias = jnp.where(first_head, bias_ref[0, 0], bias_ref[0, 1])
    other_bias = jnp.where(first_head, bias_ref[1, 0], bias_ref[1, 1])
    cached = jnp.concatenate(
        [
            jnp.broadcast_to(cached_variate_ref[s : s + 1, :], (group, piece_len))
            for s in range(slots)
        ],
        axis=0,
    )
    biases = jnp.where(variate == cached, same_bias, other_bias)
    bias_mask_ref[...] = jnp.where(iota((rows, piece_len), 1) < limit, biases, MASKED_SCORE)


def two_terms(value):
    high = value.astype(jnp.bfloat16)
    return high, (value - high.astype(jnp.float32)).astype(jnp.bfloat16)


def cache_body(
    steps,
    scale,
    arrive,
    q_ref,
    pick_ref,
    place_ref,
    same_ref,
    bias_mask_ref,
    k_ref,
    early_v_ref,
    late_v_ref,
    out_ref,
):
    slots = k_ref.shape[0]
    group = 2 * steps
    rows = slots * group
    devices = out_ref.shape[0]
    span = out_ref.shape[1] // 2
    all_queries = jnp.concatenate([q_ref[i] for i in range(devices)], axis=0)
    picked = matmul(pick_ref[...], all_queries)
    row_head = iota((rows, LANES), 0) % group // steps
    head_match = row_head == iota((rows, LANES), 1) // HD
    picked = jnp.where(head_match, picked, 0.0)
    scores = jnp.concatenate(
        [
            matmul_t(picked[group * s : group * (s + 1)].astype(jnp.bfloat16), k_ref[s])
            for s in range(slots)
        ],
        axis=0,
    )
    bias_mask = bias_mask_ref[...]
    live = bias_mask > 0.5 * MASKED_SCORE
    scores = jnp.where(live, scores * scale + bias_mask, MASKED_SCORE)
    slot_top = jnp.max(scores, axis=1, keepdims=True)
    top_lane = jnp.transpose(jnp.broadcast_to(slot_top, (rows, LANES)))[0:1, :]
    row_top = jnp.max(top_lane + same_ref[...], axis=1, keepdims=True)
    weights = jnp.where(live, jnp.exp(scores - row_top), 0.0)
    total = jnp.sum(weights, axis=1, keepdims=True)
    arrive()
    values = [r.at[i] for r in (early_v_ref, late_v_ref) for i in range(r.shape[0])]
    mixed = jnp.concatenate(
        [
            matmul(weights[group * s : group * (s + 1)].astype(jnp.bfloat16), values[s][...])
            for s in range(slots)
        ],
        axis=0,
    )
    both = jnp.concatenate(
        [jnp.where(head_match, mixed, 0.0), jnp.where(head_match, total, 0.0)], axis=1
    )
    high, low = two_terms(both)
    place = place_ref[...]
    summed = matmul(place, high) + matmul(place, low)
    out_sum, total_sum = summed[:, :LANES], summed[:, LANES:]
    lane_head = iota((1, rows), 1) % group // steps
    placed = place.astype(jnp.float32) > 0.5
    tops = [
        jnp.max(jnp.where(placed & (lane_head == h), top_lane, MASKED_SCORE), axis=1, keepdims=True)
        for h in range(2)
    ]
    low_lanes = iota(out_sum.shape, 1) < HD
    top = jnp.where(low_lanes, tops[0], tops[1])
    some = total_sum > 0.0
    safe_total = jnp.where(some, total_sum, 1.0)
    averaged = jnp.where(some, out_sum / safe_total, 0.0).astype(jnp.bfloat16)
    lse = jnp.where(some, top + jnp.log(safe_total), MASKED_SCORE)
    lse_high = lse.astype(jnp.bfloat16).astype(jnp.float32)
    rest = lse - lse_high
    lse_mid = rest.astype(jnp.bfloat16).astype(jnp.float32)
    place_in = iota(out_sum.shape, 1) % HD
    coded = jnp.where(
        place_in == 0,
        lse_high,
        jnp.where(place_in == 1, lse_mid, jnp.where(place_in == 2, rest - lse_mid, 0.0)),
    ).astype(jnp.bfloat16)
    for d in range(devices):
        out_ref[d, :span] = averaged[span * d : span * (d + 1)]
        out_ref[d, span:] = coded[span * d : span * (d + 1)]


def finish_body(arrive, part_ref, fresh_ref, fresh_lse_ref, w_ref, out_ref):
    devices = part_ref.shape[0]
    span = part_ref.shape[1] // 2
    source, lane = iota((LANES, LANES), 0), iota((LANES, LANES), 1)
    decode = jnp.where((source // HD == lane // HD) & (source % HD < 3), 1.0, 0.0)
    decode = decode.astype(jnp.bfloat16)
    lses = [matmul(part_ref[d, span:], decode) for d in range(devices)]
    top = fresh_lse_ref[...]
    for lse in lses:
        top = jnp.maximum(top, lse)
    weight = jnp.exp(fresh_lse_ref[...] - top)
    total = weight
    mixed = weight * fresh_ref[...]
    for d in range(devices):
        weight = jnp.exp(lses[d] - top)
        total = total + weight
        mixed = mixed + weight * part_ref[d, :span].astype(jnp.float32)
    attended = (mixed / total).astype(jnp.bfloat16)
    partial = matmul(attended, w_ref[...]).astype(jnp.bfloat16)
    for d in range(out_ref.shape[0]):
        out_ref[d] = partial


def gated(normed, blocks):
    low_lanes = iota((normed.shape[0], LANES), 1) < HD
    pair = jnp.concatenate([block[: normed.shape[1]] for block in blocks], axis=1)
    expanded = matmul(normed, pair)
    gates = expanded / (1.0 + jnp.exp(-expanded))
    first = gates[:, :LANES] * pltpu.roll(expanded[:, :LANES], HD, 1)
    second = pltpu.roll(gates[:, LANES:], HD, 1) * expanded[:, LANES:]
    return jnp.where(low_lanes, first, second)


def settle_body(_, part_ref, token_ref, gain_ref, normed_ref, mid_ref):
    mid = part_ref[0].astype(jnp.float32)
    for d in range(1, part_ref.shape[0]):
        mid = mid + part_ref[d].astype(jnp.float32)
    mid = mid + stacked(token_ref)
    own = mid_ref.shape[1]
    for d in range(mid_ref.shape[0]):
        mid_ref[d] = mid[own * d : own * (d + 1)]
    normed_ref[...] = scaled_rows(mid, gain_ref[...])


def feed_body(_, normed_ref, own_w_ref, near_hbm_ref, out_ref, near_w_ref, sems):
    count = near_w_ref.shape[0]
    moves = [
        pltpu.make_async_copy(near_hbm_ref.at[i], near_w_ref.at[i], sems.at[i])
        for i in range(count)
    ]
    for move in moves:
        move.start()
    own = out_ref.shape[1]
    normed = normed_ref[...]
    width = normed.shape[1]
    blocks = [r.at[i] for r in (own_w_ref, near_w_ref) for i in range(count)]
    halves = []
    for s in range(0, 2 * count, 2):
        if s >= count:
            moves[s - count].wait()
            moves[s - count + 1].wait()
        halves.append(gated(normed, blocks[s : s + 2]))
    hidden = jnp.concatenate(halves, axis=1).astype(jnp.bfloat16)
    for c in range(0, width // LANES, 2):
        at = width + HD * c
        weights = jnp.concatenate(
            [
                jnp.concatenate([block[at : at + HD], block[at + HD : at + 2 * HD]], axis=1)
                for block in blocks
            ],
            axis=0,
        )
        part = matmul(hidden, weights).astype(jnp.bfloat16)
        for d in range(out_ref.shape[0]):
            out_ref[d, :, LANES * c : LANES * (c + 2)] = part[own * d : own * (d + 1)]


def last_body(arrive, index_ref, part_ref, mid_ref, out_ref):
    total = mid_ref[index_ref[0]]
    summed = part_ref[0].astype(jnp.float32)
    for d in range(1, part_ref.shape[0]):
        summed = summed + part_ref[d].astype(jnp.float32)
    out_ref[...] = (total + summed).astype(jnp.bfloat16)


def rotation_tables(lengths, steps):
    half = HD // 2
    lane = np.arange(LANES)
    inv_freq = (10000.0 ** (-(lane % half) / half)).astype(np.float32)
    sign = np.where(lane % HD < half, -1.0, 1.0).astype(np.float32)
    offsets = jnp.arange(steps, dtype=jnp.int32)
    positions = (lengths[:, None, None] + offsets[None, :, None]).astype(jnp.float32)
    angles = positions * inv_freq
    return jnp.cos(angles), jnp.sin(angles) * sign


def on_device(
    tokens,
    w_qkv,
    w_out,
    variate_bias,
    attn_gain,
    ffn_gain,
    gate_up,
    w_down,
    cache_keys,
    cache_values,
    cache_variate,
    new_variate,
    piece_slot,
    cache_len,
):
    row_count, width = tokens.shape
    requests, steps = new_variate.shape
    slots, piece_len, lanes = cache_keys.shape
    seqs, tps = lax.axis_size("seq"), lax.axis_size("tp")
    rows = row_count * tps
    own_requests = rows // steps
    scale = 1.0 / math.sqrt(HD)
    bf16, f32 = jnp.bfloat16, jnp.float32
    shape = jax.ShapeDtypeStruct
    seq_at = lax.axis_index("seq")
    tp_at = lax.axis_index("tp").astype(jnp.int32).reshape(1)

    row_tokens = exchange(jnp.broadcast_to(tokens[None], (tps, *tokens.shape)), "tp")

    blocks, units = w_down.shape[:2]
    ffn_weights, qkv_weights, qkv_gain = kernel_call(
        pack_body,
        shape((1, width + units * width // lanes, lanes), bf16),
        [],
        "pack",
        moved=1 << 20,
        loads=[gate_up.reshape(width, lanes), w_down.reshape(units, width)],
        carried=[w_qkv.transpose(1, 0, 2), attn_gain[None, :]],
    )()
    ffn_next = swapped(ffn_weights, [2, 3, 0, 1, 6, 7, 4, 5])

    own_len = lax.dynamic_slice_in_dim(cache_len, seq_at * own_requests, own_requests, 0)
    cosine, sine = rotation_tables(own_len, steps)
    queries, keys_new, values_new = kernel_call(
        project_body,
        [shape((seqs, rows, lanes), bf16), shape((rows, lanes), bf16), shape((rows, lanes), bf16)],
        in_vmem(5),
        "project",
        moved=1 << 20,
    )(row_tokens, cosine, sine, qkv_gain, qkv_weights)
    all_queries = exchange(queries, "seq")

    slot_rows = 2 * steps * slots
    early = slots // 3
    pick, place, same, bias_mask, fresh, fresh_lse, held_values = kernel_call(
        lambda *refs: prepare_body(steps, slots, scale, *refs),
        [
            shape((slot_rows, requests * steps), bf16),
            shape((requests * steps, slot_rows), bf16),
            shape((slot_rows, slot_rows), f32),
            shape((slot_rows, piece_len), f32),
            shape((rows, lanes), f32),
            shape((rows, lanes), f32),
        ],
        in_smem(1) + in_vmem(3),
        "prepare",
        moved=1 << 20,
        loads=[piece_slot, cache_len[None, :], new_variate.T, cache_variate],
        small=[variate_bias],
        carried=[Part(cache_values, 0, early)],
        scratch=[pltpu.VMEM((requests, lanes), jnp.int32)],
    )(seq_at.astype(jnp.int32).reshape(1), queries, keys_new, values_new)

    partial = kernel_call(
        lambda *refs: cache_body(steps, scale, *refs),
        shape((seqs, 2 * rows, lanes), bf16),
        in_vmem(7),
        "cache",
        moved=4 << 20,
        loads=[Part(cache_values, early, slots - early)],
    )(all_queries, pick, place, same, bias_mask, cache_keys, held_values)
    ffn_weights, out_weights, gain = joined(
        ffn_weights, ffn_next, partial, [w_out, ffn_gain[None, :]]
    )
    partial = exchange(partial, "seq")

    ffn_far = swapped(ffn_weights, [6, 7, 4, 5, 2, 3, 0, 1])
    mid_parts = kernel_call(
        finish_body,
        shape((tps, rows, width), bf16),
        in_vmem(4),
        "finish",
        moved=30 << 20,
    )(partial, fresh, fresh_lse, out_weights)
    ffn_weights = joined(ffn_weights, ffn_far, mid_parts)
    mid_parts = exchange(mid_parts, "tp")
    ffn_near = swapped(ffn_weights, [1, 0, 3, 2, 5, 4, 7, 6])
    normed, mid = kernel_call(
        settle_body,
        [shape((rows, width), bf16), shape((tps, row_count, width), f32)],
        in_vmem(3),
        "settle",
        moved=30 << 20,
    )(mid_parts, row_tokens, gain)
    ffn_parts = kernel_call(
        feed_body,
        shape((tps, row_count, width), bf16),
        in_vmem(2) + [pl.BlockSpec(memory_space=pltpu.HBM)],
        "feed",
        moved=4 << 20,
        scratch=[
            pltpu.VMEM(ffn_near.shape, bf16),
            pltpu.SemaphoreType.DMA((ffn_near.shape[0],)),
        ],
    )(normed, ffn_weights, stay_in_hbm(ffn_near))
    ffn_parts = exchange(ffn_parts, "tp")
    return kernel_call(
        last_body, shape((row_count, width), bf16), in_smem(1) + in_vmem(2), "last", moved=1 << 17
    )(tp_at, ffn_parts, mid)


def solution(mesh):
    in_specs = (
        P(("req", "seq", "tp"), None),
        P(None, None, "tp"),
        P("tp", None),
        P(None, "tp"),
        P(),
        P(),
        P(None, ("seq", "tp"), None),
        P(("seq", "tp"), None, None),
        P(("req", "seq"), None, "tp"),
        P(("req", "seq"), None, "tp"),
        P(("req", "seq"), None),
        P("req", None),
        P("req", None),
        P("req"),
    )
    out_specs = P(("req", "seq", "tp"), None)
    return jax.shard_map(
        on_device, mesh=mesh, in_specs=in_specs, out_specs=out_specs, check_vma=False
    )
```

```python
import math

import jax
import jax.numpy as jnp
import numpy as np
from jax import lax
from jax.experimental import pallas as pl
from jax.experimental.pallas import tpu as pltpu
from jax.sharding import PartitionSpec as P

HD = 64
EPSILON = 1e-05
MASKED_SCORE = -1e30
FAR = -1e38
LANES = 128
INTERPRET = False


def exchange(pieces, axes):
    return lax.all_to_all(pieces, axes, 0, 0, tiled=True)


def swapped(blocks, partner):
    return lax.ppermute(blocks, "seq", list(enumerate(partner)))


def in_vmem(count):
    return [pl.BlockSpec(memory_space=pltpu.VMEM)] * count


def in_smem(count):
    return [pl.BlockSpec(memory_space=pltpu.SMEM)] * count


def stay_in_hbm(array):
    return array if INTERPRET else pltpu.with_memory_space_constraint(array, pltpu.HBM)


class Part:
    def __init__(self, array, start=0, size=None):
        self.array, self.start = array, start
        self.shape = (array.shape[0] if size is None else size, *array.shape[1:])
        self.dtype = array.dtype

    def of(self, ref):
        return ref if self.shape == ref.shape else ref.at[pl.ds(self.start, self.shape[0])]


def kernel_call(
    body, out_shape, in_specs, name, moved, loads=(), small=(), carried=(), scratch=()
):
    loads, small, carried = (
        [a if isinstance(a, Part) else Part(a) for a in arrays] for arrays in (loads, small, carried)
    )
    many = isinstance(out_shape, (list, tuple))
    shapes = list(out_shape) if many else [out_shape]
    outs = len(shapes)
    shapes = shapes + [jax.ShapeDtypeStruct(a.shape, a.dtype) for a in carried]
    held = [pltpu.VMEM(a.shape, a.dtype) for a in loads] + [
        pltpu.SMEM(a.shape, a.dtype) for a in small
    ]
    count, more, plain = len(held), len(carried), len(in_specs)

    def run(*refs):
        ins, refs = refs[:plain], refs[plain:]
        sources, refs = refs[: count + more], refs[count + more :]
        results, refs = refs[: outs + more], refs[outs + more :]
        buffers, refs = refs[:count], refs[count:]
        sems, rest = refs[: count + more], refs[count + more :]
        targets = [*buffers, *results[outs:]]
        sources = [a.of(ref) for a, ref in zip((*loads, *small, *carried), sources)]
        moves = [pltpu.make_async_copy(*each) for each in zip(sources, targets, sems)]
        for move in moves:
            move.start()

        def arrive(*which):
            for i in which or range(count):
                moves[i].wait()

        body(arrive, *ins, *buffers, *results[:outs], *rest)
        for move in moves[count:]:
            move.wait()

    call = pl.pallas_call(
        run,
        out_shape=shapes if many or more else shapes[0],
        in_specs=list(in_specs) + [pl.BlockSpec(memory_space=pltpu.HBM)] * (count + more),
        out_specs=in_vmem(outs + more) if many or more else in_vmem(1)[0],
        scratch_shapes=held + [pltpu.SemaphoreType.DMA(())] * (count + more) + list(scratch),
        name=name,
        interpret=INTERPRET,
        compiler_params=pltpu.CompilerParams(vmem_limit_bytes=8 << 20),
        cost_estimate=pl.CostEstimate(flops=300 * moved, bytes_accessed=moved, transcendentals=0),
    )
    return lambda *ins: call(*ins, *[stay_in_hbm(a.array) for a in (*loads, *small, *carried)])


def iota(shape, dim):
    return lax.broadcasted_iota(jnp.int32, shape, dim)


def matmul(a, b):
    return jnp.dot(a, b, preferred_element_type=jnp.float32)


def matmul_t(a, b):
    return lax.dot_general(a, b, (((1,), (1,)), ((), ())), preferred_element_type=jnp.float32)


def scaled_rows(rows, gain):
    mean_sq = jnp.mean(rows * rows, axis=-1, keepdims=True)
    return (rows * lax.rsqrt(mean_sq + EPSILON) * gain).astype(jnp.bfloat16)


def stacked(ref):
    return jnp.concatenate([ref[i].astype(jnp.float32) for i in range(ref.shape[0])], axis=0)


def pack_body(arrive, gate_ref, down_ref, out_ref):
    arrive()
    depth = gate_ref.shape[0]
    units = down_ref.shape[0]
    out_ref[0, :depth] = gate_ref[...]
    for c in range(down_ref.shape[1] // LANES):
        at = depth + units * c
        out_ref[0, at : at + units] = down_ref[:, LANES * c : LANES * (c + 1)]


def join_body(_, first_ref, second_ref, after_ref, out_ref, sem):
    count = first_ref.shape[0]
    move = pltpu.make_async_copy(second_ref, out_ref.at[pl.ds(count, count)], sem)
    move.start()
    out_ref[:count] = first_ref[...]
    move.wait()


def joined(first, second, after, carried=()):
    return kernel_call(
        join_body,
        jax.ShapeDtypeStruct((2 * first.shape[0], *first.shape[1:]), first.dtype),
        in_vmem(1) + [pl.BlockSpec(memory_space=pltpu.HBM), pl.BlockSpec(memory_space=pl.ANY)],
        "join",
        moved=4 << 20,
        carried=carried,
        scratch=[pltpu.SemaphoreType.DMA(())],
    )(first, stay_in_hbm(second), after)


def project_body(arrive, token_ref, cos_ref, sin_ref, gain_ref, w_ref, q_ref, k_ref, v_ref):
    normed = scaled_rows(stacked(token_ref), gain_ref[...])
    cosine, sine = stacked(cos_ref), stacked(sin_ref)
    first_half = iota(cosine.shape, 1) % HD < HD // 2

    def rotate(part):
        partner = jnp.where(
            first_half,
            pltpu.roll(part, LANES - HD // 2, 1),
            pltpu.roll(part, HD // 2, 1),
        )
        return (part * cosine + partner * sine).astype(jnp.bfloat16)

    queries = rotate(matmul(normed, w_ref[0]))
    for i in range(q_ref.shape[0]):
        q_ref[i] = queries
    k_ref[...] = rotate(matmul(normed, w_ref[1]))
    v_ref[...] = matmul(normed, w_ref[2]).astype(jnp.bfloat16)


def fresh_part(steps, scale, packed, q_ref, k_ref, v_ref, bias_ref, out_ref, lse_ref):
    queries = q_ref[0]
    rows = queries.shape[0]
    packed = jnp.concatenate(
        [jnp.broadcast_to(packed[i : i + 1, :rows], (steps, rows)) for i in range(packed.shape[0])],
        axis=0,
    )
    low_lanes = iota((rows, LANES), 1) < HD
    split = [
        jnp.where(low_lanes, queries, jnp.zeros_like(queries)),
        jnp.where(low_lanes, jnp.zeros_like(queries), queries),
    ]
    row_id, col_id = iota((rows, rows), 0), iota((rows, rows), 1)
    allowed = (row_id // steps == col_id // steps) & (row_id % steps >= col_id % steps)
    same = (packed >> (2 * (row_id % steps))) & 3 == (packed >> (2 * (col_id % steps))) & 3
    outs, lses = [], []
    for head in range(2):
        scores = matmul_t(split[head], k_ref[...]) * scale
        scores = scores + jnp.where(same, bias_ref[0, head], bias_ref[1, head])
        scores = jnp.where(allowed, scores, MASKED_SCORE)
        top = jnp.max(scores, axis=1, keepdims=True)
        weights = jnp.where(allowed, jnp.exp(scores - top), 0.0)
        total = jnp.sum(weights, axis=1, keepdims=True)
        outs.append(matmul(weights.astype(jnp.bfloat16), v_ref[...]) / total)
        lses.append(top + jnp.log(total))
    out_ref[...] = jnp.where(low_lanes, outs[0], outs[1])
    lse_ref[...] = jnp.where(low_lanes, lses[0], lses[1])


def prepare_body(
    steps,
    slots,
    scale,
    arrive,
    seq_ref,
    q_ref,
    k_ref,
    v_ref,
    slot_ref,
    len_ref,
    variate_ref,
    cached_variate_ref,
    bias_ref,
    pick_ref,
    place_ref,
    same_ref,
    bias_mask_ref,
    fresh_ref,
    fresh_lse_ref,
    packed_ref,
):
    requests, pieces = slot_ref.shape
    piece_len = cached_variate_ref.shape[1]
    group = 2 * steps
    rows = slots * group
    arrive()
    table = slot_ref[...]
    packed_row = variate_ref[0:1, :]
    for t in range(1, steps):
        packed_row = packed_row + (variate_ref[t : t + 1, :] << (2 * t))
    columns = jnp.where(iota((8, requests), 0) == 0, packed_row, len_ref[...])
    columns = jnp.transpose(columns.astype(jnp.float32)).astype(jnp.int32)
    packed_variate, length = columns[:, 0:1], columns[:, 1:2]
    packed_ref[...] = jnp.broadcast_to(packed_variate, (requests, LANES))
    own = requests // (requests * steps // q_ref.shape[1])
    packed = packed_ref[pl.ds(pl.multiple_of(seq_ref[0] * own, own), own), :]
    fresh_part(steps, scale, packed, q_ref, k_ref, v_ref, bias_ref, fresh_ref, fresh_lse_ref)

    live = jnp.clip(length - piece_len * iota((requests, pieces), 1), 0, piece_len)
    code = (iota((requests, pieces), 0) << 17) + (packed_variate << 9) + live
    code = code.astype(jnp.float32)
    base = seq_ref[0] * slots
    found = []
    for s in range(slots):
        hit = jnp.where(table == base + s, code, -1.0)
        hit = jnp.max(jnp.max(hit, axis=0, keepdims=True), axis=1, keepdims=True)
        found.append(jnp.broadcast_to(hit, (group, LANES)))
    found = jnp.concatenate(found, axis=0)
    found_lane = jnp.transpose(found)[0:1, :].astype(jnp.int32)
    found = found[:, 0:1].astype(jnp.int32)
    owned = found >= 0
    owner = jnp.where(owned, found >> 17, -1)
    owner_lane = jnp.where(found_lane >= 0, found_lane >> 17, -1)
    row_in = iota((rows, 1), 0) % group
    step_row = row_in % steps
    lane_in = iota((1, rows), 1) % group

    wide = (rows, requests * steps)
    pick_ref[...] = jnp.where(
        iota(wide, 1) == jnp.where(owned, owner * steps + step_row, -1), 1.0, 0.0
    ).astype(jnp.bfloat16)
    tall = (requests * steps, rows)
    place_ref[...] = jnp.where(
        iota(tall, 0) == jnp.where(owner_lane >= 0, owner_lane * steps + lane_in % steps, -1),
        1.0,
        0.0,
    ).astype(jnp.bfloat16)
    same_ref[...] = jnp.where(
        (owner == owner_lane) & (row_in == lane_in), 0.0, FAR
    ).astype(jnp.bfloat16)

    limit = jnp.where(owned, found & 511, 0)
    variate = (found >> (9 + 2 * step_row)) & 3
    first_head = row_in < steps
    same_bias = jnp.where(first_head, bias_ref[0, 0], bias_ref[0, 1])
    other_bias = jnp.where(first_head, bias_ref[1, 0], bias_ref[1, 1])
    cached = jnp.concatenate(
        [
            jnp.broadcast_to(cached_variate_ref[s : s + 1, :], (group, piece_len))
            for s in range(slots)
        ],
        axis=0,
    )
    biases = jnp.where(variate == cached, same_bias, other_bias)
    bias_mask_ref[...] = jnp.where(iota((rows, piece_len), 1) < limit, biases, MASKED_SCORE)


def two_terms(value):
    high = value.astype(jnp.bfloat16)
    return high, (value - high.astype(jnp.float32)).astype(jnp.bfloat16)


def cache_body(
    steps,
    scale,
    arrive,
    q_ref,
    pick_ref,
    place_ref,
    same_ref,
    bias_mask_ref,
    k_ref,
    early_v_ref,
    late_v_ref,
    out_ref,
):
    slots = k_ref.shape[0]
    group = 2 * steps
    rows = slots * group
    devices = out_ref.shape[0]
    span = out_ref.shape[1] // 2
    all_queries = jnp.concatenate([q_ref[i] for i in range(devices)], axis=0)
    picked = matmul(pick_ref[...], all_queries)
    row_head = iota((rows, LANES), 0) % group // steps
    head_match = row_head == iota((rows, LANES), 1) // HD
    picked = jnp.where(head_match, picked, 0.0)
    scores = jnp.concatenate(
        [
            matmul_t(picked[group * s : group * (s + 1)].astype(jnp.bfloat16), k_ref[s])
            for s in range(slots)
        ],
        axis=0,
    )
    bias_mask = bias_mask_ref[...]
    live = bias_mask > 0.5 * MASKED_SCORE
    scores = jnp.where(live, scores * scale + bias_mask, MASKED_SCORE)
    slot_top = jnp.max(scores, axis=1, keepdims=True)
    top_lane = jnp.transpose(jnp.broadcast_to(slot_top, (rows, LANES)))[0:1, :]
    row_top = jnp.max(top_lane + same_ref[...].astype(jnp.float32), axis=1, keepdims=True)
    weights = jnp.where(live, jnp.exp(scores - row_top), 0.0)
    total = jnp.sum(weights, axis=1, keepdims=True)
    arrive()
    values = [r.at[i] for r in (early_v_ref, late_v_ref) for i in range(r.shape[0])]
    mixed = jnp.concatenate(
        [
            matmul(weights[group * s : group * (s + 1)].astype(jnp.bfloat16), values[s][...])
            for s in range(slots)
        ],
        axis=0,
    )
    both = jnp.concatenate(
        [jnp.where(head_match, mixed, 0.0), jnp.where(head_match, total, 0.0)], axis=1
    )
    high, low = two_terms(both)
    place = place_ref[...]
    summed = matmul(place, high) + matmul(place, low)
    out_sum, total_sum = summed[:, :LANES], summed[:, LANES:]
    lane_head = iota((1, rows), 1) % group // steps
    placed = place.astype(jnp.float32) > 0.5
    tops = [
        jnp.max(jnp.where(placed & (lane_head == h), top_lane, MASKED_SCORE), axis=1, keepdims=True)
        for h in range(2)
    ]
    low_lanes = iota(out_sum.shape, 1) < HD
    top = jnp.where(low_lanes, tops[0], tops[1])
    some = total_sum > 0.0
    safe_total = jnp.where(some, total_sum, 1.0)
    averaged = jnp.where(some, out_sum / safe_total, 0.0).astype(jnp.bfloat16)
    lse = jnp.where(some, top + jnp.log(safe_total), MASKED_SCORE)
    lse_high = lse.astype(jnp.bfloat16).astype(jnp.float32)
    rest = lse - lse_high
    lse_mid = rest.astype(jnp.bfloat16).astype(jnp.float32)
    place_in = iota(out_sum.shape, 1) % HD
    coded = jnp.where(
        place_in == 0,
        lse_high,
        jnp.where(place_in == 1, lse_mid, jnp.where(place_in == 2, rest - lse_mid, 0.0)),
    ).astype(jnp.bfloat16)
    for d in range(devices):
        out_ref[d, :span] = averaged[span * d : span * (d + 1)]
        out_ref[d, span:] = coded[span * d : span * (d + 1)]


def finish_body(arrive, part_ref, fresh_ref, fresh_lse_ref, w_ref, out_ref):
    devices = part_ref.shape[0]
    span = part_ref.shape[1] // 2
    source, lane = iota((LANES, LANES), 0), iota((LANES, LANES), 1)
    decode = jnp.where((source // HD == lane // HD) & (source % HD < 3), 1.0, 0.0)
    decode = decode.astype(jnp.bfloat16)
    lses = [matmul(part_ref[d, span:], decode) for d in range(devices)]
    top = fresh_lse_ref[...]
    for lse in lses:
        top = jnp.maximum(top, lse)
    weight = jnp.exp(fresh_lse_ref[...] - top)
    total = weight
    mixed = weight * fresh_ref[...]
    for d in range(devices):
        weight = jnp.exp(lses[d] - top)
        total = total + weight
        mixed = mixed + weight * part_ref[d, :span].astype(jnp.float32)
    attended = (mixed / total).astype(jnp.bfloat16)
    partial = matmul(attended, w_ref[...]).astype(jnp.bfloat16)
    for d in range(out_ref.shape[0]):
        out_ref[d] = partial


def gated(normed, blocks):
    low_lanes = iota((normed.shape[0], LANES), 1) < HD
    pair = jnp.concatenate([block[: normed.shape[1]] for block in blocks], axis=1)
    expanded = matmul(normed, pair)
    gates = expanded / (1.0 + jnp.exp(-expanded))
    first = gates[:, :LANES] * pltpu.roll(expanded[:, :LANES], HD, 1)
    second = pltpu.roll(gates[:, LANES:], HD, 1) * expanded[:, LANES:]
    return jnp.where(low_lanes, first, second)


def settle_body(_, part_ref, token_ref, gain_ref, normed_ref, mid_ref):
    mid = part_ref[0].astype(jnp.float32)
    for d in range(1, part_ref.shape[0]):
        mid = mid + part_ref[d].astype(jnp.float32)
    mid = mid + stacked(token_ref)
    own = mid_ref.shape[1]
    for d in range(mid_ref.shape[0]):
        mid_ref[d] = mid[own * d : own * (d + 1)]
    normed_ref[...] = scaled_rows(mid, gain_ref[...])


def feed_body(_, normed_ref, own_w_ref, near_hbm_ref, out_ref, near_w_ref, sems):
    count = near_w_ref.shape[0]
    moves = [
        pltpu.make_async_copy(near_hbm_ref.at[i], near_w_ref.at[i], sems.at[i])
        for i in range(count)
    ]
    for move in moves:
        move.start()
    own = out_ref.shape[1]
    normed = normed_ref[...]
    width = normed.shape[1]
    blocks = [r.at[i] for r in (own_w_ref, near_w_ref) for i in range(count)]
    halves = []
    for s in range(0, 2 * count, 2):
        if s >= count:
            moves[s - count].wait()
            moves[s - count + 1].wait()
        halves.append(gated(normed, blocks[s : s + 2]))
    hidden = jnp.concatenate(halves, axis=1).astype(jnp.bfloat16)
    for c in range(0, width // LANES, 2):
        at = width + HD * c
        weights = jnp.concatenate(
            [
                jnp.concatenate([block[at : at + HD], block[at + HD : at + 2 * HD]], axis=1)
                for block in blocks
            ],
            axis=0,
        )
        part = matmul(hidden, weights).astype(jnp.bfloat16)
        for d in range(out_ref.shape[0]):
            out_ref[d, :, LANES * c : LANES * (c + 2)] = part[own * d : own * (d + 1)]


def last_body(arrive, index_ref, part_ref, mid_ref, out_ref):
    total = mid_ref[index_ref[0]]
    summed = part_ref[0].astype(jnp.float32)
    for d in range(1, part_ref.shape[0]):
        summed = summed + part_ref[d].astype(jnp.float32)
    out_ref[...] = (total + summed).astype(jnp.bfloat16)


def rotation_tables(lengths, steps):
    half = HD // 2
    lane = np.arange(LANES)
    inv_freq = (10000.0 ** (-(lane % half) / half)).astype(np.float32)
    sign = np.where(lane % HD < half, -1.0, 1.0).astype(np.float32)
    offsets = jnp.arange(steps, dtype=jnp.int32)
    positions = (lengths[:, None, None] + offsets[None, :, None]).astype(jnp.float32)
    angles = positions * inv_freq
    return jnp.cos(angles), jnp.sin(angles) * sign


def on_device(
    tokens,
    w_qkv,
    w_out,
    variate_bias,
    attn_gain,
    ffn_gain,
    gate_up,
    w_down,
    cache_keys,
    cache_values,
    cache_variate,
    new_variate,
    piece_slot,
    cache_len,
):
    row_count, width = tokens.shape
    requests, steps = new_variate.shape
    slots, piece_len, lanes = cache_keys.shape
    seqs, tps = lax.axis_size("seq"), lax.axis_size("tp")
    rows = row_count * tps
    own_requests = rows // steps
    scale = 1.0 / math.sqrt(HD)
    bf16, f32 = jnp.bfloat16, jnp.float32
    shape = jax.ShapeDtypeStruct
    seq_at = lax.axis_index("seq")
    tp_at = lax.axis_index("tp").astype(jnp.int32).reshape(1)

    row_tokens = exchange(jnp.broadcast_to(tokens[None], (tps, *tokens.shape)), "tp")

    blocks, units = w_down.shape[:2]
    ffn_weights, qkv_weights, qkv_gain = kernel_call(
        pack_body,
        shape((1, width + units * width // lanes, lanes), bf16),
        [],
        "pack",
        moved=1 << 20,
        loads=[gate_up.reshape(width, lanes), w_down.reshape(units, width)],
        carried=[w_qkv.transpose(1, 0, 2), attn_gain[None, :]],
    )()
    ffn_next = swapped(ffn_weights, [2, 7, 0, 5, 6, 3, 4, 1])

    own_len = lax.dynamic_slice_in_dim(cache_len, seq_at * own_requests, own_requests, 0)
    cosine, sine = rotation_tables(own_len, steps)
    queries, keys_new, values_new = kernel_call(
        project_body,
        [shape((seqs, rows, lanes), bf16), shape((rows, lanes), bf16), shape((rows, lanes), bf16)],
        in_vmem(5),
        "project",
        moved=1 << 20,
    )(row_tokens, cosine, sine, qkv_gain, qkv_weights)
    all_queries = exchange(queries, "seq")

    slot_rows = 2 * steps * slots
    early = slots // 2
    pick, place, same, bias_mask, fresh, fresh_lse, held_values = kernel_call(
        lambda *refs: prepare_body(steps, slots, scale, *refs),
        [
            shape((slot_rows, requests * steps), bf16),
            shape((requests * steps, slot_rows), bf16),
            shape((slot_rows, slot_rows), bf16),
            shape((slot_rows, piece_len), f32),
            shape((rows, lanes), f32),
            shape((rows, lanes), f32),
        ],
        in_smem(1) + in_vmem(3),
        "prepare",
        moved=1 << 20,
        loads=[piece_slot, cache_len[None, :], new_variate.T, cache_variate],
        small=[variate_bias],
        carried=[Part(cache_values, 0, early)],
        scratch=[pltpu.VMEM((requests, lanes), jnp.int32)],
    )(seq_at.astype(jnp.int32).reshape(1), queries, keys_new, values_new)

    partial = kernel_call(
        lambda *refs: cache_body(steps, scale, *refs),
        shape((seqs, 2 * rows, lanes), bf16),
        in_vmem(7),
        "cache",
        moved=4 << 20,
        loads=[Part(cache_values, early, slots - early)],
    )(all_queries, pick, place, same, bias_mask, cache_keys, held_values)
    ffn_weights, out_weights, gain = joined(
        ffn_weights, ffn_next, partial, [w_out, ffn_gain[None, :]]
    )
    partial = exchange(partial, "seq")

    ffn_far = swapped(ffn_weights, [6, 3, 4, 1, 2, 7, 0, 5])
    mid_parts = kernel_call(
        finish_body,
        shape((tps, rows, width), bf16),
        in_vmem(4),
        "finish",
        moved=30 << 20,
    )(partial, fresh, fresh_lse, out_weights)
    ffn_weights = joined(ffn_weights, ffn_far, mid_parts)
    mid_parts = exchange(mid_parts, "tp")
    ffn_near = swapped(ffn_weights, [1, 0, 3, 2, 5, 4, 7, 6])
    normed, mid = kernel_call(
        settle_body,
        [shape((rows, width), bf16), shape((tps, row_count, width), f32)],
        in_vmem(3),
        "settle",
        moved=30 << 20,
    )(mid_parts, row_tokens, gain)
    ffn_parts = kernel_call(
        feed_body,
        shape((tps, row_count, width), bf16),
        in_vmem(2) + [pl.BlockSpec(memory_space=pltpu.HBM)],
        "feed",
        moved=4 << 20,
        scratch=[
            pltpu.VMEM(ffn_near.shape, bf16),
            pltpu.SemaphoreType.DMA((ffn_near.shape[0],)),
        ],
    )(normed, ffn_weights, stay_in_hbm(ffn_near))
    ffn_parts = exchange(ffn_parts, "tp")
    return kernel_call(
        last_body, shape((row_count, width), bf16), in_smem(1) + in_vmem(2), "last", moved=1 << 17
    )(tp_at, ffn_parts, mid)


def solution(mesh):
    in_specs = (
        P(("req", "seq", "tp"), None),
        P(None, None, "tp"),
        P("tp", None),
        P(None, "tp"),
        P(),
        P(),
        P(None, ("seq", "tp"), None),
        P(("seq", "tp"), None, None),
        P(("req", "seq"), None, "tp"),
        P(("req", "seq"), None, "tp"),
        P(("req", "seq"), None),
        P("req", None),
        P("req", None),
        P("req"),
    )
    out_specs = P(("req", "seq", "tp"), None)
    return jax.shard_map(
        on_device, mesh=mesh, in_specs=in_specs, out_specs=out_specs, check_vma=False
    )
```

```python
import math

import jax
import jax.numpy as jnp
import numpy as np
from jax import lax
from jax.experimental import pallas as pl
from jax.experimental.pallas import tpu as pltpu
from jax.sharding import PartitionSpec as P

HD = 64
EPSILON = 1e-05
MASKED_SCORE = -1e30
FAR = -1e38
LANES = 128
INTERPRET = False


def exchange(pieces, axes):
    return lax.all_to_all(pieces, axes, 0, 0, tiled=True)


def swapped(blocks, partner):
    return lax.ppermute(blocks, "seq", list(enumerate(partner)))


def in_vmem(count):
    return [pl.BlockSpec(memory_space=pltpu.VMEM)] * count


def in_smem(count):
    return [pl.BlockSpec(memory_space=pltpu.SMEM)] * count


def stay_in_hbm(array):
    return array if INTERPRET else pltpu.with_memory_space_constraint(array, pltpu.HBM)


class Part:
    def __init__(self, array, start=0, size=None):
        self.array, self.start = array, start
        self.shape = (array.shape[0] if size is None else size, *array.shape[1:])
        self.dtype = array.dtype

    def of(self, ref):
        return ref if self.shape == ref.shape else ref.at[pl.ds(self.start, self.shape[0])]


def kernel_call(
    body, out_shape, in_specs, name, moved, loads=(), small=(), carried=(), scratch=()
):
    loads, small, carried = (
        [a if isinstance(a, Part) else Part(a) for a in arrays] for arrays in (loads, small, carried)
    )
    many = isinstance(out_shape, (list, tuple))
    shapes = list(out_shape) if many else [out_shape]
    outs = len(shapes)
    shapes = shapes + [jax.ShapeDtypeStruct(a.shape, a.dtype) for a in carried]
    held = [pltpu.VMEM(a.shape, a.dtype) for a in loads] + [
        pltpu.SMEM(a.shape, a.dtype) for a in small
    ]
    count, more, plain = len(held), len(carried), len(in_specs)

    def run(*refs):
        ins, refs = refs[:plain], refs[plain:]
        sources, refs = refs[: count + more], refs[count + more :]
        results, refs = refs[: outs + more], refs[outs + more :]
        buffers, refs = refs[:count], refs[count:]
        sems, rest = refs[: count + more], refs[count + more :]
        targets = [*buffers, *results[outs:]]
        sources = [a.of(ref) for a, ref in zip((*loads, *small, *carried), sources)]
        moves = [pltpu.make_async_copy(*each) for each in zip(sources, targets, sems)]
        for move in moves:
            move.start()

        def arrive(*which):
            for i in which or range(count):
                moves[i].wait()

        body(arrive, *ins, *buffers, *results[:outs], *rest)
        for move in moves[count:]:
            move.wait()

    call = pl.pallas_call(
        run,
        out_shape=shapes if many or more else shapes[0],
        in_specs=list(in_specs) + [pl.BlockSpec(memory_space=pltpu.HBM)] * (count + more),
        out_specs=in_vmem(outs + more) if many or more else in_vmem(1)[0],
        scratch_shapes=held + [pltpu.SemaphoreType.DMA(())] * (count + more) + list(scratch),
        name=name,
        interpret=INTERPRET,
        compiler_params=pltpu.CompilerParams(vmem_limit_bytes=8 << 20),
        cost_estimate=pl.CostEstimate(flops=300 * moved, bytes_accessed=moved, transcendentals=0),
    )
    return lambda *ins: call(*ins, *[stay_in_hbm(a.array) for a in (*loads, *small, *carried)])


def iota(shape, dim):
    return lax.broadcasted_iota(jnp.int32, shape, dim)


def matmul(a, b):
    return jnp.dot(a, b, preferred_element_type=jnp.float32)


def matmul_t(a, b):
    return lax.dot_general(a, b, (((1,), (1,)), ((), ())), preferred_element_type=jnp.float32)


def scaled_rows(rows, gain):
    mean_sq = jnp.mean(rows * rows, axis=-1, keepdims=True)
    return (rows * lax.rsqrt(mean_sq + EPSILON) * gain).astype(jnp.bfloat16)


def stacked(ref):
    return jnp.concatenate([ref[i].astype(jnp.float32) for i in range(ref.shape[0])], axis=0)


def pack_body(arrive, gate_ref, down_ref, out_ref):
    arrive()
    depth = gate_ref.shape[0]
    units = down_ref.shape[0]
    out_ref[0, :depth] = gate_ref[...]
    for c in range(down_ref.shape[1] // LANES):
        at = depth + units * c
        out_ref[0, at : at + units] = down_ref[:, LANES * c : LANES * (c + 1)]


def join_body(_, first_ref, second_ref, after_ref, out_ref, sem):
    count = first_ref.shape[0]
    move = pltpu.make_async_copy(second_ref, out_ref.at[pl.ds(count, count)], sem)
    move.start()
    out_ref[:count] = first_ref[...]
    move.wait()


def joined(first, second, after, carried=()):
    return kernel_call(
        join_body,
        jax.ShapeDtypeStruct((2 * first.shape[0], *first.shape[1:]), first.dtype),
        in_vmem(1) + [pl.BlockSpec(memory_space=pltpu.HBM), pl.BlockSpec(memory_space=pl.ANY)],
        "join",
        moved=4 << 20,
        carried=carried,
        scratch=[pltpu.SemaphoreType.DMA(())],
    )(first, stay_in_hbm(second), after)


def extend_body(_, first_ref, far_ref, after_ref, out_ref, held_ref, last_ref, sems):
    count = first_ref.shape[0]
    kept = held_ref.shape[0]
    far = [
        pltpu.make_async_copy(far_ref.at[pl.ds(0, kept)], held_ref, sems.at[0]),
        pltpu.make_async_copy(far_ref.at[pl.ds(kept, kept)], last_ref, sems.at[1]),
    ]
    out = [
        pltpu.make_async_copy(first_ref, out_ref.at[pl.ds(0, count)], sems.at[2]),
        pltpu.make_async_copy(held_ref, out_ref.at[pl.ds(count, kept)], sems.at[3]),
        pltpu.make_async_copy(last_ref, out_ref.at[pl.ds(count + kept, kept)], sems.at[4]),
    ]
    for move in (*far, out[0]):
        move.start()
    for i in range(2):
        far[i].wait()
        out[i + 1].start()
    for move in out:
        move.wait()


def extended(first, far, after):
    count, kept = first.shape[0], far.shape[0] // 2
    return pl.pallas_call(
        lambda *refs: extend_body(None, *refs),
        out_shape=[
            jax.ShapeDtypeStruct((2 * count, *first.shape[1:]), first.dtype),
            jax.ShapeDtypeStruct((kept, *first.shape[1:]), first.dtype),
        ],
        in_specs=in_vmem(1)
        + [pl.BlockSpec(memory_space=pltpu.HBM), pl.BlockSpec(memory_space=pl.ANY)],
        out_specs=[pl.BlockSpec(memory_space=pltpu.HBM), *in_vmem(1)],
        scratch_shapes=[
            pltpu.VMEM((kept, *first.shape[1:]), first.dtype),
            pltpu.SemaphoreType.DMA((5,)),
        ],
        name="extend",
        interpret=INTERPRET,
        compiler_params=pltpu.CompilerParams(vmem_limit_bytes=8 << 20),
        cost_estimate=pl.CostEstimate(
            flops=300 * 4 << 20, bytes_accessed=4 << 20, transcendentals=0
        ),
    )(first, stay_in_hbm(far), after)


def project_body(arrive, token_ref, cos_ref, sin_ref, gain_ref, w_ref, q_ref, k_ref, v_ref):
    normed = scaled_rows(stacked(token_ref), gain_ref[...])
    cosine, sine = stacked(cos_ref), stacked(sin_ref)
    first_half = iota(cosine.shape, 1) % HD < HD // 2

    def rotate(part):
        partner = jnp.where(
            first_half,
            pltpu.roll(part, LANES - HD // 2, 1),
            pltpu.roll(part, HD // 2, 1),
        )
        return (part * cosine + partner * sine).astype(jnp.bfloat16)

    queries = rotate(matmul(normed, w_ref[0]))
    for i in range(q_ref.shape[0]):
        q_ref[i] = queries
    k_ref[...] = rotate(matmul(normed, w_ref[1]))
    v_ref[...] = matmul(normed, w_ref[2]).astype(jnp.bfloat16)


def fresh_part(steps, scale, packed, q_ref, k_ref, v_ref, bias_ref, out_ref, lse_ref):
    queries = q_ref[0]
    rows = queries.shape[0]
    packed = jnp.concatenate(
        [jnp.broadcast_to(packed[i : i + 1, :rows], (steps, rows)) for i in range(packed.shape[0])],
        axis=0,
    )
    low_lanes = iota((rows, LANES), 1) < HD
    split = [
        jnp.where(low_lanes, queries, jnp.zeros_like(queries)),
        jnp.where(low_lanes, jnp.zeros_like(queries), queries),
    ]
    row_id, col_id = iota((rows, rows), 0), iota((rows, rows), 1)
    allowed = (row_id // steps == col_id // steps) & (row_id % steps >= col_id % steps)
    same = (packed >> (2 * (row_id % steps))) & 3 == (packed >> (2 * (col_id % steps))) & 3
    outs, lses = [], []
    for head in range(2):
        scores = matmul_t(split[head], k_ref[...]) * scale
        scores = scores + jnp.where(same, bias_ref[0, head], bias_ref[1, head])
        scores = jnp.where(allowed, scores, MASKED_SCORE)
        top = jnp.max(scores, axis=1, keepdims=True)
        weights = jnp.where(allowed, jnp.exp(scores - top), 0.0)
        total = jnp.sum(weights, axis=1, keepdims=True)
        outs.append(matmul(weights.astype(jnp.bfloat16), v_ref[...]) / total)
        lses.append(top + jnp.log(total))
    out_ref[...] = jnp.where(low_lanes, outs[0], outs[1])
    lse_ref[...] = jnp.where(low_lanes, lses[0], lses[1])


def prepare_body(
    steps,
    slots,
    scale,
    arrive,
    seq_ref,
    q_ref,
    k_ref,
    v_ref,
    slot_ref,
    len_ref,
    variate_ref,
    cached_variate_ref,
    bias_ref,
    pick_ref,
    place_ref,
    same_ref,
    bias_mask_ref,
    fresh_ref,
    fresh_lse_ref,
    packed_ref,
):
    requests, pieces = slot_ref.shape
    piece_len = cached_variate_ref.shape[1]
    group = 2 * steps
    rows = slots * group
    arrive()
    table = slot_ref[...]
    packed_row = variate_ref[0:1, :]
    for t in range(1, steps):
        packed_row = packed_row + (variate_ref[t : t + 1, :] << (2 * t))
    columns = jnp.where(iota((8, requests), 0) == 0, packed_row, len_ref[...])
    columns = jnp.transpose(columns.astype(jnp.float32)).astype(jnp.int32)
    packed_variate, length = columns[:, 0:1], columns[:, 1:2]
    packed_ref[...] = jnp.broadcast_to(packed_variate, (requests, LANES))
    own = requests // (requests * steps // q_ref.shape[1])
    packed = packed_ref[pl.ds(pl.multiple_of(seq_ref[0] * own, own), own), :]
    fresh_part(steps, scale, packed, q_ref, k_ref, v_ref, bias_ref, fresh_ref, fresh_lse_ref)

    live = jnp.clip(length - piece_len * iota((requests, pieces), 1), 0, piece_len)
    code = (iota((requests, pieces), 0) << 17) + (packed_variate << 9) + live
    code = code.astype(jnp.float32)
    base = seq_ref[0] * slots
    found = []
    for s in range(slots):
        hit = jnp.where(table == base + s, code, -1.0)
        hit = jnp.max(jnp.max(hit, axis=0, keepdims=True), axis=1, keepdims=True)
        found.append(jnp.broadcast_to(hit, (group, LANES)))
    found = jnp.concatenate(found, axis=0)
    found_lane = jnp.transpose(found)[0:1, :].astype(jnp.int32)
    found = found[:, 0:1].astype(jnp.int32)
    owned = found >= 0
    owner = jnp.where(owned, found >> 17, -1)
    owner_lane = jnp.where(found_lane >= 0, found_lane >> 17, -1)
    row_in = iota((rows, 1), 0) % group
    step_row = row_in % steps
    lane_in = iota((1, rows), 1) % group

    wide = (rows, requests * steps)
    pick_ref[...] = jnp.where(
        iota(wide, 1) == jnp.where(owned, owner * steps + step_row, -1), 1.0, 0.0
    ).astype(jnp.bfloat16)
    tall = (requests * steps, rows)
    place_ref[...] = jnp.where(
        iota(tall, 0) == jnp.where(owner_lane >= 0, owner_lane * steps + lane_in % steps, -1),
        1.0,
        0.0,
    ).astype(jnp.bfloat16)
    same_ref[...] = jnp.where(
        (owner == owner_lane) & (row_in == lane_in), 0.0, FAR
    ).astype(jnp.bfloat16)

    limit = jnp.where(owned, found & 511, 0)
    variate = (found >> (9 + 2 * step_row)) & 3
    first_head = row_in < steps
    same_bias = jnp.where(first_head, bias_ref[0, 0], bias_ref[0, 1])
    other_bias = jnp.where(first_head, bias_ref[1, 0], bias_ref[1, 1])
    cached = jnp.concatenate(
        [
            jnp.broadcast_to(cached_variate_ref[s : s + 1, :], (group, piece_len))
            for s in range(slots)
        ],
        axis=0,
    )
    biases = jnp.where(variate == cached, same_bias, other_bias)
    bias_mask_ref[...] = jnp.where(iota((rows, piece_len), 1) < limit, biases, MASKED_SCORE)


def two_terms(value):
    high = value.astype(jnp.bfloat16)
    return high, (value - high.astype(jnp.float32)).astype(jnp.bfloat16)


def cache_body(
    steps,
    scale,
    arrive,
    q_ref,
    pick_ref,
    place_ref,
    same_ref,
    bias_mask_ref,
    k_ref,
    early_v_ref,
    late_v_ref,
    out_ref,
):
    slots = k_ref.shape[0]
    group = 2 * steps
    rows = slots * group
    devices = out_ref.shape[0]
    span = out_ref.shape[1] // 2
    all_queries = jnp.concatenate([q_ref[i] for i in range(devices)], axis=0)
    picked = matmul(pick_ref[...], all_queries)
    row_head = iota((rows, LANES), 0) % group // steps
    head_match = row_head == iota((rows, LANES), 1) // HD
    picked = jnp.where(head_match, picked, 0.0)
    doubled = jnp.concatenate([picked, picked], axis=1)
    wide = doubled.shape
    own_half = iota(wide, 0) // group % 2 == iota(wide, 1) // LANES
    doubled = jnp.where(own_half, doubled, 0.0).astype(jnp.bfloat16)
    scores = jnp.concatenate(
        [
            matmul_t(
                doubled[group * s : group * (s + 2)],
                jnp.concatenate([k_ref[s], k_ref[s + 1]], axis=1),
            )
            for s in range(0, slots, 2)
        ],
        axis=0,
    )
    bias_mask = bias_mask_ref[...]
    live = bias_mask > 0.5 * MASKED_SCORE
    scores = jnp.where(live, scores * scale + bias_mask, MASKED_SCORE)
    slot_top = jnp.max(scores, axis=1, keepdims=True)
    by_slot = jnp.where(pick_ref[...].astype(jnp.float32) > 0.5, slot_top, MASKED_SCORE)
    tops = by_slot[:group]
    for s in range(1, slots):
        tops = jnp.maximum(tops, by_slot[group * s : group * (s + 1)])
    tops = jnp.where(
        iota(tops.shape, 0) == 0,
        jnp.max(tops[:steps], axis=0, keepdims=True),
        jnp.max(tops[steps:], axis=0, keepdims=True),
    )
    tops = jnp.transpose(tops)
    top_lane = jnp.transpose(jnp.broadcast_to(slot_top, (rows, LANES)))[0:1, :]
    row_top = jnp.max(top_lane + same_ref[...].astype(jnp.float32), axis=1, keepdims=True)
    weights = jnp.where(live, jnp.exp(scores - row_top), 0.0)
    total = jnp.sum(weights, axis=1, keepdims=True)
    arrive()
    values = [r.at[i] for r in (early_v_ref, late_v_ref) for i in range(r.shape[0])]
    weights = weights.astype(jnp.bfloat16)
    mixed = jnp.concatenate(
        [
            matmul(
                weights[group * s : group * (s + 2)],
                jnp.concatenate([values[s][...], values[s + 1][...]], axis=1),
            )
            for s in range(0, slots, 2)
        ],
        axis=0,
    )
    mixed = jnp.where(iota(mixed.shape, 0) // group % 2 == iota(mixed.shape, 1) // LANES, mixed, 0.0)
    mixed = mixed[:, :LANES] + mixed[:, LANES:]
    both = jnp.concatenate(
        [jnp.where(head_match, mixed, 0.0), jnp.where(head_match, total, 0.0)], axis=1
    )
    high, low = two_terms(both)
    place = place_ref[...]
    summed = matmul(place, high) + matmul(place, low)
    out_sum, total_sum = summed[:, :LANES], summed[:, LANES:]
    low_lanes = iota(out_sum.shape, 1) < HD
    top = jnp.where(low_lanes, tops[:, 0:1], tops[:, 1:2])
    some = total_sum > 0.0
    safe_total = jnp.where(some, total_sum, 1.0)
    averaged = jnp.where(some, out_sum / safe_total, 0.0).astype(jnp.bfloat16)
    lse = jnp.where(some, top + jnp.log(safe_total), MASKED_SCORE)
    lse_high = lse.astype(jnp.bfloat16).astype(jnp.float32)
    rest = lse - lse_high
    lse_mid = rest.astype(jnp.bfloat16).astype(jnp.float32)
    place_in = iota(out_sum.shape, 1) % HD
    coded = jnp.where(
        place_in == 0,
        lse_high,
        jnp.where(place_in == 1, lse_mid, jnp.where(place_in == 2, rest - lse_mid, 0.0)),
    ).astype(jnp.bfloat16)
    for d in range(devices):
        out_ref[d, :span] = averaged[span * d : span * (d + 1)]
        out_ref[d, span:] = coded[span * d : span * (d + 1)]


def finish_body(arrive, part_ref, fresh_ref, fresh_lse_ref, w_ref, out_ref):
    devices = part_ref.shape[0]
    span = part_ref.shape[1] // 2
    source, lane = iota((LANES, LANES), 0), iota((LANES, LANES), 1)
    decode = jnp.where((source // HD == lane // HD) & (source % HD < 3), 1.0, 0.0)
    decode = decode.astype(jnp.bfloat16)
    lses = [matmul(part_ref[d, span:], decode) for d in range(devices)]
    top = fresh_lse_ref[...]
    for lse in lses:
        top = jnp.maximum(top, lse)
    weight = jnp.exp(fresh_lse_ref[...] - top)
    total = weight
    mixed = weight * fresh_ref[...]
    for d in range(devices):
        weight = jnp.exp(lses[d] - top)
        total = total + weight
        mixed = mixed + weight * part_ref[d, :span].astype(jnp.float32)
    attended = (mixed / total).astype(jnp.bfloat16)
    partial = matmul(attended, w_ref[...]).astype(jnp.bfloat16)
    for d in range(out_ref.shape[0]):
        out_ref[d] = partial


def gated(normed, blocks):
    low_lanes = iota((normed.shape[0], LANES), 1) < HD
    pair = jnp.concatenate([block[: normed.shape[1]] for block in blocks], axis=1)
    expanded = matmul(normed, pair)
    gates = expanded / (1.0 + jnp.exp(-expanded))
    first = gates[:, :LANES] * pltpu.roll(expanded[:, :LANES], HD, 1)
    second = pltpu.roll(gates[:, LANES:], HD, 1) * expanded[:, LANES:]
    return jnp.where(low_lanes, first, second)


def settle_body(_, part_ref, token_ref, gain_ref, normed_ref, mid_ref):
    mid = part_ref[0].astype(jnp.float32)
    for d in range(1, part_ref.shape[0]):
        mid = mid + part_ref[d].astype(jnp.float32)
    mid = mid + stacked(token_ref)
    own = mid_ref.shape[1]
    for d in range(mid_ref.shape[0]):
        mid_ref[d] = mid[own * d : own * (d + 1)]
    normed_ref[...] = scaled_rows(mid, gain_ref[...])


def feed_body(_, normed_ref, own_w_ref, near_w_ref, held_w_ref, far_ref, out_ref, last_w_ref, sem):
    move = pltpu.make_async_copy(
        far_ref.at[pl.ds(held_w_ref.shape[0], last_w_ref.shape[0])], last_w_ref, sem
    )
    move.start()
    own = out_ref.shape[1]
    normed = normed_ref[...]
    width = normed.shape[1]
    refs = (own_w_ref, near_w_ref, held_w_ref, last_w_ref)
    blocks = [r.at[i] for r in refs for i in range(r.shape[0])]
    halves = []
    for s in range(0, len(blocks), 2):
        if s + 2 == len(blocks):
            move.wait()
        halves.append(gated(normed, blocks[s : s + 2]))
    hidden = jnp.concatenate(halves, axis=1).astype(jnp.bfloat16)
    for c in range(0, width // LANES, 2):
        at = width + HD * c
        weights = jnp.concatenate(
            [
                jnp.concatenate([block[at : at + HD], block[at + HD : at + 2 * HD]], axis=1)
                for block in blocks
            ],
            axis=0,
        )
        part = matmul(hidden, weights).astype(jnp.bfloat16)
        for d in range(out_ref.shape[0]):
            out_ref[d, :, LANES * c : LANES * (c + 2)] = part[own * d : own * (d + 1)]


def last_body(arrive, index_ref, part_ref, mid_ref, out_ref):
    total = mid_ref[index_ref[0]]
    summed = part_ref[0].astype(jnp.float32)
    for d in range(1, part_ref.shape[0]):
        summed = summed + part_ref[d].astype(jnp.float32)
    out_ref[...] = (total + summed).astype(jnp.bfloat16)


def rotation_tables(lengths, steps):
    half = HD // 2
    lane = np.arange(LANES)
    inv_freq = (10000.0 ** (-(lane % half) / half)).astype(np.float32)
    sign = np.where(lane % HD < half, -1.0, 1.0).astype(np.float32)
    offsets = jnp.arange(steps, dtype=jnp.int32)
    positions = (lengths[:, None, None] + offsets[None, :, None]).astype(jnp.float32)
    angles = positions * inv_freq
    return jnp.cos(angles), jnp.sin(angles) * sign


def on_device(
    tokens,
    w_qkv,
    w_out,
    variate_bias,
    attn_gain,
    ffn_gain,
    gate_up,
    w_down,
    cache_keys,
    cache_values,
    cache_variate,
    new_variate,
    piece_slot,
    cache_len,
):
    row_count, width = tokens.shape
    requests, steps = new_variate.shape
    slots, piece_len, lanes = cache_keys.shape
    seqs, tps = lax.axis_size("seq"), lax.axis_size("tp")
    rows = row_count * tps
    own_requests = rows // steps
    scale = 1.0 / math.sqrt(HD)
    bf16, f32 = jnp.bfloat16, jnp.float32
    shape = jax.ShapeDtypeStruct
    seq_at = lax.axis_index("seq")
    tp_at = lax.axis_index("tp").astype(jnp.int32).reshape(1)

    row_tokens = exchange(jnp.broadcast_to(tokens[None], (tps, *tokens.shape)), "tp")

    blocks, units = w_down.shape[:2]
    ffn_weights, qkv_weights, qkv_gain = kernel_call(
        pack_body,
        shape((1, width + units * width // lanes, lanes), bf16),
        [],
        "pack",
        moved=1 << 20,
        loads=[gate_up.reshape(width, lanes), w_down.reshape(units, width)],
        carried=[w_qkv.transpose(1, 0, 2), attn_gain[None, :]],
    )()
    ffn_next = swapped(ffn_weights, [2, 7, 0, 5, 6, 3, 4, 1])

    own_len = lax.dynamic_slice_in_dim(cache_len, seq_at * own_requests, own_requests, 0)
    cosine, sine = rotation_tables(own_len, steps)
    queries, keys_new, values_new = kernel_call(
        project_body,
        [shape((seqs, rows, lanes), bf16), shape((rows, lanes), bf16), shape((rows, lanes), bf16)],
        in_vmem(5),
        "project",
        moved=1 << 20,
    )(row_tokens, cosine, sine, qkv_gain, qkv_weights)
    all_queries = exchange(queries, "seq")

    slot_rows = 2 * steps * slots
    early = slots // 2
    pick, place, same, bias_mask, fresh, fresh_lse, held_values = kernel_call(
        lambda *refs: prepare_body(steps, slots, scale, *refs),
        [
            shape((slot_rows, requests * steps), bf16),
            shape((requests * steps, slot_rows), bf16),
            shape((slot_rows, slot_rows), bf16),
            shape((slot_rows, piece_len), f32),
            shape((rows, lanes), f32),
            shape((rows, lanes), f32),
        ],
        in_smem(1) + in_vmem(3),
        "prepare",
        moved=1 << 20,
        loads=[piece_slot, cache_len[None, :], new_variate.T, cache_variate],
        small=[variate_bias],
        carried=[Part(cache_values, 0, early)],
        scratch=[pltpu.VMEM((requests, lanes), jnp.int32)],
    )(seq_at.astype(jnp.int32).reshape(1), queries, keys_new, values_new)

    partial = kernel_call(
        lambda *refs: cache_body(steps, scale, *refs),
        shape((seqs, 2 * rows, lanes), bf16),
        in_vmem(7),
        "cache",
        moved=4 << 20,
        loads=[Part(cache_values, early, slots - early)],
    )(all_queries, pick, place, same, bias_mask, cache_keys, held_values)
    ffn_weights, out_weights, gain = joined(
        ffn_weights, ffn_next, partial, [w_out, ffn_gain[None, :]]
    )
    partial = exchange(partial, "seq")

    ffn_far = swapped(ffn_weights, [6, 3, 4, 1, 2, 7, 0, 5])
    mid_parts = kernel_call(
        finish_body,
        shape((tps, rows, width), bf16),
        in_vmem(4),
        "finish",
        moved=30 << 20,
    )(partial, fresh, fresh_lse, out_weights)
    ffn_all, ffn_held = extended(ffn_weights, ffn_far, mid_parts)
    mid_parts = exchange(mid_parts, "tp")
    ffn_near = swapped(ffn_all, [1, 0, 3, 2, 5, 4, 7, 6])
    normed, mid = kernel_call(
        settle_body,
        [shape((rows, width), bf16), shape((tps, row_count, width), f32)],
        in_vmem(3),
        "settle",
        moved=30 << 20,
    )(mid_parts, row_tokens, gain)
    ffn_parts = kernel_call(
        feed_body,
        shape((tps, row_count, width), bf16),
        in_vmem(4) + [pl.BlockSpec(memory_space=pltpu.HBM)],
        "feed",
        moved=4 << 20,
        scratch=[pltpu.VMEM(ffn_held.shape, bf16), pltpu.SemaphoreType.DMA(())],
    )(normed, ffn_weights, ffn_near, ffn_held, stay_in_hbm(ffn_far))
    ffn_parts = exchange(ffn_parts, "tp")
    return kernel_call(
        last_body, shape((row_count, width), bf16), in_smem(1) + in_vmem(2), "last", moved=1 << 17
    )(tp_at, ffn_parts, mid)


def solution(mesh):
    in_specs = (
        P(("req", "seq", "tp"), None),
        P(None, None, "tp"),
        P("tp", None),
        P(None, "tp"),
        P(),
        P(),
        P(None, ("seq", "tp"), None),
        P(("seq", "tp"), None, None),
        P(("req", "seq"), None, "tp"),
        P(("req", "seq"), None, "tp"),
        P(("req", "seq"), None),
        P("req", None),
        P("req", None),
        P("req"),
    )
    out_specs = P(("req", "seq", "tp"), None)
    return jax.shard_map(
        on_device, mesh=mesh, in_specs=in_specs, out_specs=out_specs, check_vma=False
    )
```

```python
import math

import jax
import jax.numpy as jnp
import numpy as np
from jax import lax
from jax.experimental import pallas as pl
from jax.experimental.pallas import tpu as pltpu
from jax.sharding import PartitionSpec as P

HD = 64
EPSILON = 1e-05
MASKED_SCORE = -1e30
FAR = -1e38
LANES = 128
INTERPRET = False


def exchange(pieces, axes):
    return lax.all_to_all(pieces, axes, 0, 0, tiled=True)


def swapped(blocks, partner):
    return lax.ppermute(blocks, "seq", list(enumerate(partner)))


def in_vmem(count):
    return [pl.BlockSpec(memory_space=pltpu.VMEM)] * count


def in_smem(count):
    return [pl.BlockSpec(memory_space=pltpu.SMEM)] * count


def stay_in_hbm(array):
    return array if INTERPRET else pltpu.with_memory_space_constraint(array, pltpu.HBM)


class Part:
    def __init__(self, array, start=0, size=None):
        self.array, self.start = array, start
        self.shape = (array.shape[0] if size is None else size, *array.shape[1:])
        self.dtype = array.dtype

    def of(self, ref):
        return ref if self.shape == ref.shape else ref.at[pl.ds(self.start, self.shape[0])]


def kernel_call(
    body, out_shape, in_specs, name, moved, loads=(), small=(), carried=(), scratch=(), spread=False
):
    loads, small, carried = (
        [a if isinstance(a, Part) else Part(a) for a in arrays] for arrays in (loads, small, carried)
    )
    many = isinstance(out_shape, (list, tuple))
    shapes = list(out_shape) if many else [out_shape]
    outs = len(shapes)
    shapes = shapes + [jax.ShapeDtypeStruct(a.shape, a.dtype) for a in carried]
    held = [pltpu.VMEM(a.shape, a.dtype) for a in loads] + [
        pltpu.SMEM(a.shape, a.dtype) for a in small
    ]
    count, more, plain = len(held), len(carried), len(in_specs)

    def run(*refs):
        ins, refs = refs[:plain], refs[plain:]
        sources, refs = refs[: count + more], refs[count + more :]
        results, refs = refs[: outs + more], refs[outs + more :]
        buffers, refs = refs[:count], refs[count:]
        sems, rest = refs[: count + more], refs[count + more :]
        targets = [*buffers, *results[outs:]]
        sources = [a.of(ref) for a, ref in zip((*loads, *small, *carried), sources)]
        moves = [pltpu.make_async_copy(*each) for each in zip(sources, targets, sems)]
        for move in moves:
            move.start()

        def arrive(*which):
            for i in which or range(count):
                moves[i].wait()

        body(arrive, *ins, *buffers, *results[:outs], *rest)
        for move in moves[count:]:
            move.wait()

    places = in_vmem(outs + more)
    if spread:
        places[0] = pl.BlockSpec(memory_space=pltpu.HBM)
    call = pl.pallas_call(
        run,
        out_shape=shapes if many or more else shapes[0],
        in_specs=list(in_specs) + [pl.BlockSpec(memory_space=pltpu.HBM)] * (count + more),
        out_specs=places if many or more else places[0],
        scratch_shapes=held + [pltpu.SemaphoreType.DMA(())] * (count + more) + list(scratch),
        name=name,
        interpret=INTERPRET,
        compiler_params=pltpu.CompilerParams(vmem_limit_bytes=8 << 20),
        cost_estimate=pl.CostEstimate(flops=300 * moved, bytes_accessed=moved, transcendentals=0),
    )
    return lambda *ins: call(*ins, *[stay_in_hbm(a.array) for a in (*loads, *small, *carried)])


def iota(shape, dim):
    return lax.broadcasted_iota(jnp.int32, shape, dim)


def matmul(a, b):
    return jnp.dot(a, b, preferred_element_type=jnp.float32)


def matmul_t(a, b):
    return lax.dot_general(a, b, (((1,), (1,)), ((), ())), preferred_element_type=jnp.float32)


def scaled_rows(rows, gain):
    mean_sq = jnp.mean(rows * rows, axis=-1, keepdims=True)
    return (rows * lax.rsqrt(mean_sq + EPSILON) * gain).astype(jnp.bfloat16)


def stacked(ref):
    return jnp.concatenate([ref[i].astype(jnp.float32) for i in range(ref.shape[0])], axis=0)


def pack_body(arrive, gate_ref, down_ref, out_ref):
    arrive()
    depth = gate_ref.shape[0]
    units = down_ref.shape[0]
    out_ref[0, :depth] = gate_ref[...]
    for c in range(down_ref.shape[1] // LANES):
        at = depth + units * c
        out_ref[0, at : at + units] = down_ref[:, LANES * c : LANES * (c + 1)]


def join_body(_, first_ref, second_ref, after_ref, out_ref, sem):
    count = first_ref.shape[0]
    move = pltpu.make_async_copy(second_ref, out_ref.at[pl.ds(count, count)], sem)
    move.start()
    out_ref[:count] = first_ref[...]
    move.wait()


def joined(first, second, after, carried=()):
    return kernel_call(
        join_body,
        jax.ShapeDtypeStruct((2 * first.shape[0], *first.shape[1:]), first.dtype),
        in_vmem(1) + [pl.BlockSpec(memory_space=pltpu.HBM), pl.BlockSpec(memory_space=pl.ANY)],
        "join",
        moved=4 << 20,
        carried=carried,
        scratch=[pltpu.SemaphoreType.DMA(())],
    )(first, stay_in_hbm(second), after)


def extend_body(_, first_ref, far_ref, after_ref, out_ref, held_ref, last_ref, sems):
    count = first_ref.shape[0]
    kept = held_ref.shape[0]
    far = [
        pltpu.make_async_copy(far_ref.at[pl.ds(0, kept)], held_ref, sems.at[0]),
        pltpu.make_async_copy(far_ref.at[pl.ds(kept, kept)], last_ref, sems.at[1]),
    ]
    out = [
        pltpu.make_async_copy(first_ref, out_ref.at[pl.ds(0, count)], sems.at[2]),
        pltpu.make_async_copy(held_ref, out_ref.at[pl.ds(count, kept)], sems.at[3]),
        pltpu.make_async_copy(last_ref, out_ref.at[pl.ds(count + kept, kept)], sems.at[4]),
    ]
    for move in (*far, out[0]):
        move.start()
    for i in range(2):
        far[i].wait()
        out[i + 1].start()
    for move in out:
        move.wait()


def extended(first, far, after):
    count, kept = first.shape[0], far.shape[0] // 2
    return pl.pallas_call(
        lambda *refs: extend_body(None, *refs),
        out_shape=[
            jax.ShapeDtypeStruct((2 * count, *first.shape[1:]), first.dtype),
            jax.ShapeDtypeStruct((kept, *first.shape[1:]), first.dtype),
        ],
        in_specs=in_vmem(1)
        + [pl.BlockSpec(memory_space=pltpu.HBM), pl.BlockSpec(memory_space=pl.ANY)],
        out_specs=[pl.BlockSpec(memory_space=pltpu.HBM), *in_vmem(1)],
        scratch_shapes=[
            pltpu.VMEM((kept, *first.shape[1:]), first.dtype),
            pltpu.SemaphoreType.DMA((5,)),
        ],
        name="extend",
        interpret=INTERPRET,
        compiler_params=pltpu.CompilerParams(vmem_limit_bytes=8 << 20),
        cost_estimate=pl.CostEstimate(
            flops=300 * 4 << 20, bytes_accessed=4 << 20, transcendentals=0
        ),
    )(first, stay_in_hbm(far), after)


def repeats(block_ref, out_ref, sems):
    moves = [
        pltpu.make_async_copy(block_ref, out_ref.at[i], sems.at[i]) for i in range(out_ref.shape[0])
    ]
    for move in moves:
        move.start()
    return moves


def project_body(
    _, token_ref, cos_ref, sin_ref, gain_ref, w_ref, q_ref, own_q_ref, k_ref, v_ref, sems
):
    normed = scaled_rows(stacked(token_ref), gain_ref[...])
    cosine, sine = stacked(cos_ref), stacked(sin_ref)
    first_half = iota(cosine.shape, 1) % HD < HD // 2

    def rotate(part):
        partner = jnp.where(
            first_half,
            pltpu.roll(part, LANES - HD // 2, 1),
            pltpu.roll(part, HD // 2, 1),
        )
        return (part * cosine + partner * sine).astype(jnp.bfloat16)

    own_q_ref[...] = rotate(matmul(normed, w_ref[0]))
    moves = repeats(own_q_ref, q_ref, sems)
    k_ref[...] = rotate(matmul(normed, w_ref[1]))
    v_ref[...] = matmul(normed, w_ref[2]).astype(jnp.bfloat16)
    for move in moves:
        move.wait()


def fresh_part(steps, scale, packed, q_ref, k_ref, v_ref, bias_ref, out_ref, lse_ref):
    queries = q_ref[...]
    rows = queries.shape[0]
    packed = jnp.concatenate(
        [jnp.broadcast_to(packed[i : i + 1, :rows], (steps, rows)) for i in range(packed.shape[0])],
        axis=0,
    )
    low_lanes = iota((rows, LANES), 1) < HD
    split = [
        jnp.where(low_lanes, queries, jnp.zeros_like(queries)),
        jnp.where(low_lanes, jnp.zeros_like(queries), queries),
    ]
    row_id, col_id = iota((rows, rows), 0), iota((rows, rows), 1)
    allowed = (row_id // steps == col_id // steps) & (row_id % steps >= col_id % steps)
    same = (packed >> (2 * (row_id % steps))) & 3 == (packed >> (2 * (col_id % steps))) & 3
    outs, lses = [], []
    for head in range(2):
        scores = matmul_t(split[head], k_ref[...]) * scale
        scores = scores + jnp.where(same, bias_ref[0, head], bias_ref[1, head])
        scores = jnp.where(allowed, scores, MASKED_SCORE)
        top = jnp.max(scores, axis=1, keepdims=True)
        weights = jnp.where(allowed, jnp.exp(scores - top), 0.0)
        total = jnp.sum(weights, axis=1, keepdims=True)
        outs.append(matmul(weights.astype(jnp.bfloat16), v_ref[...]) / total)
        lses.append(top + jnp.log(total))
    out_ref[...] = jnp.where(low_lanes, outs[0], outs[1])
    lse_ref[...] = jnp.where(low_lanes, lses[0], lses[1])


def prepare_body(
    steps,
    slots,
    scale,
    arrive,
    seq_ref,
    q_ref,
    k_ref,
    v_ref,
    slot_ref,
    len_ref,
    variate_ref,
    cached_variate_ref,
    bias_ref,
    pick_ref,
    place_ref,
    same_ref,
    bias_mask_ref,
    fresh_ref,
    fresh_lse_ref,
    packed_ref,
):
    requests, pieces = slot_ref.shape
    piece_len = cached_variate_ref.shape[1]
    group = 2 * steps
    rows = slots * group
    arrive()
    table = slot_ref[...]
    packed_row = variate_ref[0:1, :]
    for t in range(1, steps):
        packed_row = packed_row + (variate_ref[t : t + 1, :] << (2 * t))
    columns = jnp.where(iota((8, requests), 0) == 0, packed_row, len_ref[...])
    columns = jnp.transpose(columns.astype(jnp.float32)).astype(jnp.int32)
    packed_variate, length = columns[:, 0:1], columns[:, 1:2]
    packed_ref[...] = jnp.broadcast_to(packed_variate, (requests, LANES))
    own = requests // (requests * steps // q_ref.shape[0])
    packed = packed_ref[pl.ds(pl.multiple_of(seq_ref[0] * own, own), own), :]
    fresh_part(steps, scale, packed, q_ref, k_ref, v_ref, bias_ref, fresh_ref, fresh_lse_ref)

    live = jnp.clip(length - piece_len * iota((requests, pieces), 1), 0, piece_len)
    code = (iota((requests, pieces), 0) << 17) + (packed_variate << 9) + live
    code = code.astype(jnp.float32)
    base = seq_ref[0] * slots
    found = []
    for s in range(slots):
        hit = jnp.where(table == base + s, code, -1.0)
        hit = jnp.max(jnp.max(hit, axis=0, keepdims=True), axis=1, keepdims=True)
        found.append(jnp.broadcast_to(hit, (group, LANES)))
    found = jnp.concatenate(found, axis=0)
    found_lane = jnp.transpose(found)[0:1, :].astype(jnp.int32)
    found = found[:, 0:1].astype(jnp.int32)
    owned = found >= 0
    owner = jnp.where(owned, found >> 17, -1)
    owner_lane = jnp.where(found_lane >= 0, found_lane >> 17, -1)
    row_in = iota((rows, 1), 0) % group
    step_row = row_in % steps
    lane_in = iota((1, rows), 1) % group

    wide = (rows, requests * steps)
    pick_ref[...] = jnp.where(
        iota(wide, 1) == jnp.where(owned, owner * steps + step_row, -1), 1.0, 0.0
    ).astype(jnp.bfloat16)
    tall = (requests * steps, rows)
    place_ref[...] = jnp.where(
        iota(tall, 0) == jnp.where(owner_lane >= 0, owner_lane * steps + lane_in % steps, -1),
        1.0,
        0.0,
    ).astype(jnp.bfloat16)
    same_ref[...] = jnp.where(
        (owner == owner_lane) & (row_in == lane_in), 0.0, FAR
    ).astype(jnp.bfloat16)

    limit = jnp.where(owned, found & 511, 0)
    variate = (found >> (9 + 2 * step_row)) & 3
    first_head = row_in < steps
    same_bias = jnp.where(first_head, bias_ref[0, 0], bias_ref[0, 1])
    other_bias = jnp.where(first_head, bias_ref[1, 0], bias_ref[1, 1])
    cached = jnp.concatenate(
        [
            jnp.broadcast_to(cached_variate_ref[s : s + 1, :], (group, piece_len))
            for s in range(slots)
        ],
        axis=0,
    )
    biases = jnp.where(variate == cached, same_bias, other_bias)
    bias_mask_ref[...] = jnp.where(iota((rows, piece_len), 1) < limit, biases, MASKED_SCORE)


def two_terms(value):
    high = value.astype(jnp.bfloat16)
    return high, (value - high.astype(jnp.float32)).astype(jnp.bfloat16)


def cache_body(
    steps,
    scale,
    arrive,
    q_ref,
    pick_ref,
    place_ref,
    same_ref,
    bias_mask_ref,
    k_ref,
    early_v_ref,
    late_v_ref,
    out_ref,
):
    slots = k_ref.shape[0]
    group = 2 * steps
    rows = slots * group
    devices = out_ref.shape[0]
    span = out_ref.shape[1] // 2
    all_queries = jnp.concatenate([q_ref[i] for i in range(devices)], axis=0)
    picked = matmul(pick_ref[...], all_queries)
    row_head = iota((rows, LANES), 0) % group // steps
    head_match = row_head == iota((rows, LANES), 1) // HD
    picked = jnp.where(head_match, picked, 0.0)
    doubled = jnp.concatenate([picked, picked], axis=1)
    wide = doubled.shape
    own_half = iota(wide, 0) // group % 2 == iota(wide, 1) // LANES
    doubled = jnp.where(own_half, doubled, 0.0).astype(jnp.bfloat16)
    scores = jnp.concatenate(
        [
            matmul_t(
                doubled[group * s : group * (s + 2)],
                jnp.concatenate([k_ref[s], k_ref[s + 1]], axis=1),
            )
            for s in range(0, slots, 2)
        ],
        axis=0,
    )
    bias_mask = bias_mask_ref[...]
    live = bias_mask > 0.5 * MASKED_SCORE
    scores = jnp.where(live, scores * scale + bias_mask, MASKED_SCORE)
    slot_top = jnp.max(scores, axis=1, keepdims=True)
    by_slot = jnp.where(pick_ref[...].astype(jnp.float32) > 0.5, slot_top, MASKED_SCORE)
    tops = by_slot[:group]
    for s in range(1, slots):
        tops = jnp.maximum(tops, by_slot[group * s : group * (s + 1)])
    tops = jnp.where(
        iota(tops.shape, 0) == 0,
        jnp.max(tops[:steps], axis=0, keepdims=True),
        jnp.max(tops[steps:], axis=0, keepdims=True),
    )
    tops = jnp.transpose(tops)
    top_lane = jnp.transpose(jnp.broadcast_to(slot_top, (rows, LANES)))[0:1, :]
    row_top = jnp.max(top_lane + same_ref[...].astype(jnp.float32), axis=1, keepdims=True)
    weights = jnp.where(live, jnp.exp(scores - row_top), 0.0)
    total = jnp.sum(weights, axis=1, keepdims=True)
    arrive()
    values = [r.at[i] for r in (early_v_ref, late_v_ref) for i in range(r.shape[0])]
    weights = weights.astype(jnp.bfloat16)
    mixed = jnp.concatenate(
        [
            matmul(
                weights[group * s : group * (s + 2)],
                jnp.concatenate([values[s][...], values[s + 1][...]], axis=1),
            )
            for s in range(0, slots, 2)
        ],
        axis=0,
    )
    mixed = jnp.where(iota(mixed.shape, 0) // group % 2 == iota(mixed.shape, 1) // LANES, mixed, 0.0)
    mixed = mixed[:, :LANES] + mixed[:, LANES:]
    both = jnp.concatenate(
        [jnp.where(head_match, mixed, 0.0), jnp.where(head_match, total, 0.0)], axis=1
    )
    high, low = two_terms(both)
    place = place_ref[...]
    half = place.shape[0] // 2
    summed = jnp.concatenate(
        [matmul(p, high) + matmul(p, low) for p in (place[:half], place[half:])], axis=0
    )
    out_sum, total_sum = summed[:, :LANES], summed[:, LANES:]
    low_lanes = iota(out_sum.shape, 1) < HD
    top = jnp.where(low_lanes, tops[:, 0:1], tops[:, 1:2])
    some = total_sum > 0.0
    safe_total = jnp.where(some, total_sum, 1.0)
    averaged = jnp.where(some, out_sum / safe_total, 0.0).astype(jnp.bfloat16)
    lse = jnp.where(some, top + jnp.log(safe_total), MASKED_SCORE)
    lse_high = lse.astype(jnp.bfloat16).astype(jnp.float32)
    rest = lse - lse_high
    lse_mid = rest.astype(jnp.bfloat16).astype(jnp.float32)
    place_in = iota(out_sum.shape, 1) % HD
    coded = jnp.where(
        place_in == 0,
        lse_high,
        jnp.where(place_in == 1, lse_mid, jnp.where(place_in == 2, rest - lse_mid, 0.0)),
    ).astype(jnp.bfloat16)
    for d in range(devices):
        out_ref[d, :span] = averaged[span * d : span * (d + 1)]
        out_ref[d, span:] = coded[span * d : span * (d + 1)]


def finish_body(_, part_ref, fresh_ref, fresh_lse_ref, w_ref, out_ref, sum_ref, sems):
    devices = part_ref.shape[0]
    span = part_ref.shape[1] // 2
    source, lane = iota((LANES, LANES), 0), iota((LANES, LANES), 1)
    decode = jnp.where((source // HD == lane // HD) & (source % HD < 3), 1.0, 0.0)
    decode = decode.astype(jnp.bfloat16)
    lses = [matmul(part_ref[d, span:], decode) for d in range(devices)]
    top = fresh_lse_ref[...]
    for lse in lses:
        top = jnp.maximum(top, lse)
    weight = jnp.exp(fresh_lse_ref[...] - top)
    total = weight
    mixed = weight * fresh_ref[...]
    for d in range(devices):
        weight = jnp.exp(lses[d] - top)
        total = total + weight
        mixed = mixed + weight * part_ref[d, :span].astype(jnp.float32)
    attended = (mixed / total).astype(jnp.bfloat16)
    sum_ref[...] = matmul(attended, w_ref[...]).astype(jnp.bfloat16)
    for move in repeats(sum_ref, out_ref, sems):
        move.wait()


def gated(normed, blocks):
    low_lanes = iota((normed.shape[0], LANES), 1) < HD
    pair = jnp.concatenate([block[: normed.shape[1]] for block in blocks], axis=1)
    expanded = matmul(normed, pair)
    gates = expanded / (1.0 + jnp.exp(-expanded))
    first = gates[:, :LANES] * pltpu.roll(expanded[:, :LANES], HD, 1)
    second = pltpu.roll(gates[:, LANES:], HD, 1) * expanded[:, LANES:]
    return jnp.where(low_lanes, first, second)


def settle_body(_, part_ref, token_ref, gain_ref, normed_ref, mid_ref):
    mid = part_ref[0].astype(jnp.float32)
    for d in range(1, part_ref.shape[0]):
        mid = mid + part_ref[d].astype(jnp.float32)
    mid = mid + stacked(token_ref)
    own = mid_ref.shape[1]
    for d in range(mid_ref.shape[0]):
        mid_ref[d] = mid[own * d : own * (d + 1)]
    normed_ref[...] = scaled_rows(mid, gain_ref[...])


def feed_body(_, normed_ref, own_w_ref, near_w_ref, held_w_ref, far_ref, out_ref, last_w_ref, sem):
    move = pltpu.make_async_copy(
        far_ref.at[pl.ds(held_w_ref.shape[0], last_w_ref.shape[0])], last_w_ref, sem
    )
    move.start()
    own = out_ref.shape[1]
    normed = normed_ref[...]
    width = normed.shape[1]
    refs = (own_w_ref, near_w_ref, held_w_ref, last_w_ref)
    blocks = [r.at[i] for r in refs for i in range(r.shape[0])]
    halves = []
    for s in range(0, len(blocks), 2):
        if s + 2 == len(blocks):
            move.wait()
        halves.append(gated(normed, blocks[s : s + 2]))
    hidden = jnp.concatenate(halves, axis=1).astype(jnp.bfloat16)
    for c in range(0, width // LANES, 2):
        at = width + HD * c
        weights = jnp.concatenate(
            [
                jnp.concatenate([block[at : at + HD], block[at + HD : at + 2 * HD]], axis=1)
                for block in blocks
            ],
            axis=0,
        )
        part = matmul(hidden, weights).astype(jnp.bfloat16)
        for d in range(out_ref.shape[0]):
            out_ref[d, :, LANES * c : LANES * (c + 2)] = part[own * d : own * (d + 1)]


def last_body(arrive, index_ref, part_ref, mid_ref, out_ref):
    total = mid_ref[index_ref[0]]
    summed = part_ref[0].astype(jnp.float32)
    for d in range(1, part_ref.shape[0]):
        summed = summed + part_ref[d].astype(jnp.float32)
    out_ref[...] = (total + summed).astype(jnp.bfloat16)


def rotation_tables(lengths, steps):
    half = HD // 2
    lane = np.arange(LANES)
    inv_freq = (10000.0 ** (-(lane % half) / half)).astype(np.float32)
    sign = np.where(lane % HD < half, -1.0, 1.0).astype(np.float32)
    offsets = jnp.arange(steps, dtype=jnp.int32)
    positions = (lengths[:, None, None] + offsets[None, :, None]).astype(jnp.float32)
    angles = positions * inv_freq
    return jnp.cos(angles), jnp.sin(angles) * sign


def on_device(
    tokens,
    w_qkv,
    w_out,
    variate_bias,
    attn_gain,
    ffn_gain,
    gate_up,
    w_down,
    cache_keys,
    cache_values,
    cache_variate,
    new_variate,
    piece_slot,
    cache_len,
):
    row_count, width = tokens.shape
    requests, steps = new_variate.shape
    slots, piece_len, lanes = cache_keys.shape
    seqs, tps = lax.axis_size("seq"), lax.axis_size("tp")
    rows = row_count * tps
    own_requests = rows // steps
    scale = 1.0 / math.sqrt(HD)
    bf16, f32 = jnp.bfloat16, jnp.float32
    shape = jax.ShapeDtypeStruct
    seq_at = lax.axis_index("seq")
    tp_at = lax.axis_index("tp").astype(jnp.int32).reshape(1)

    row_tokens = exchange(jnp.broadcast_to(tokens[None], (tps, *tokens.shape)), "tp")

    blocks, units = w_down.shape[:2]
    ffn_weights, qkv_weights, qkv_gain = kernel_call(
        pack_body,
        shape((1, width + units * width // lanes, lanes), bf16),
        [],
        "pack",
        moved=1 << 20,
        loads=[gate_up.reshape(width, lanes), w_down.reshape(units, width)],
        carried=[w_qkv.transpose(1, 0, 2), attn_gain[None, :]],
    )()
    ffn_next = swapped(ffn_weights, [2, 7, 0, 5, 6, 3, 4, 1])

    own_len = lax.dynamic_slice_in_dim(cache_len, seq_at * own_requests, own_requests, 0)
    cosine, sine = rotation_tables(own_len, steps)
    queries, own_queries, keys_new, values_new = kernel_call(
        project_body,
        [shape((seqs, rows, lanes), bf16)] + [shape((rows, lanes), bf16)] * 3,
        in_vmem(5),
        "project",
        moved=1 << 20,
        scratch=[pltpu.SemaphoreType.DMA((seqs,))],
        spread=True,
    )(row_tokens, cosine, sine, qkv_gain, qkv_weights)
    all_queries = exchange(queries, "seq")

    slot_rows = 2 * steps * slots
    early = slots // 2
    pick, place, same, bias_mask, fresh, fresh_lse, held_values = kernel_call(
        lambda *refs: prepare_body(steps, slots, scale, *refs),
        [
            shape((slot_rows, requests * steps), bf16),
            shape((requests * steps, slot_rows), bf16),
            shape((slot_rows, slot_rows), bf16),
            shape((slot_rows, piece_len), f32),
            shape((rows, lanes), f32),
            shape((rows, lanes), f32),
        ],
        in_smem(1) + in_vmem(3),
        "prepare",
        moved=1 << 20,
        loads=[piece_slot, cache_len[None, :], new_variate.T, cache_variate],
        small=[variate_bias],
        carried=[Part(cache_values, 0, early)],
        scratch=[pltpu.VMEM((requests, lanes), jnp.int32)],
    )(seq_at.astype(jnp.int32).reshape(1), own_queries, keys_new, values_new)

    partial = kernel_call(
        lambda *refs: cache_body(steps, scale, *refs),
        shape((seqs, 2 * rows, lanes), bf16),
        in_vmem(7),
        "cache",
        moved=4 << 20,
        loads=[Part(cache_values, early, slots - early)],
    )(all_queries, pick, place, same, bias_mask, cache_keys, held_values)
    ffn_weights, out_weights, gain = joined(
        ffn_weights, ffn_next, partial, [w_out, ffn_gain[None, :]]
    )
    partial = exchange(partial, "seq")

    ffn_far = swapped(ffn_weights, [6, 3, 4, 1, 2, 7, 0, 5])
    mid_parts = kernel_call(
        finish_body,
        shape((tps, rows, width), bf16),
        in_vmem(4),
        "finish",
        moved=30 << 20,
        scratch=[pltpu.VMEM((rows, width), bf16), pltpu.SemaphoreType.DMA((tps,))],
        spread=True,
    )(partial, fresh, fresh_lse, out_weights)
    ffn_all, ffn_held = extended(ffn_weights, ffn_far, mid_parts)
    mid_parts = exchange(mid_parts, "tp")
    ffn_near = swapped(ffn_all, [1, 0, 3, 2, 5, 4, 7, 6])
    normed, mid = kernel_call(
        settle_body,
        [shape((rows, width), bf16), shape((tps, row_count, width), f32)],
        in_vmem(3),
        "settle",
        moved=30 << 20,
    )(mid_parts, row_tokens, gain)
    ffn_parts = kernel_call(
        feed_body,
        shape((tps, row_count, width), bf16),
        in_vmem(4) + [pl.BlockSpec(memory_space=pltpu.HBM)],
        "feed",
        moved=4 << 20,
        scratch=[pltpu.VMEM(ffn_held.shape, bf16), pltpu.SemaphoreType.DMA(())],
    )(normed, ffn_weights, ffn_near, ffn_held, stay_in_hbm(ffn_far))
    ffn_parts = exchange(ffn_parts, "tp")
    return kernel_call(
        last_body, shape((row_count, width), bf16), in_smem(1) + in_vmem(2), "last", moved=1 << 17
    )(tp_at, ffn_parts, mid)


def solution(mesh):
    in_specs = (
        P(("req", "seq", "tp"), None),
        P(None, None, "tp"),
        P("tp", None),
        P(None, "tp"),
        P(),
        P(),
        P(None, ("seq", "tp"), None),
        P(("seq", "tp"), None, None),
        P(("req", "seq"), None, "tp"),
        P(("req", "seq"), None, "tp"),
        P(("req", "seq"), None),
        P("req", None),
        P("req", None),
        P("req"),
    )
    out_specs = P(("req", "seq", "tp"), None)
    return jax.shard_map(
        on_device, mesh=mesh, in_specs=in_specs, out_specs=out_specs, check_vma=False
    )
```

```python
import math

import jax
import jax.numpy as jnp
import numpy as np
from jax import lax
from jax.experimental import pallas as pl
from jax.experimental.pallas import tpu as pltpu
from jax.sharding import PartitionSpec as P

HD = 64
EPSILON = 1e-05
MASKED_SCORE = -1e30
FAR = -1e38
LANES = 128
INTERPRET = False


def exchange(pieces, axes):
    return lax.all_to_all(pieces, axes, 0, 0, tiled=True)


def swapped(blocks, partner):
    return lax.ppermute(blocks, "seq", list(enumerate(partner)))


def in_vmem(count):
    return [pl.BlockSpec(memory_space=pltpu.VMEM)] * count


def in_smem(count):
    return [pl.BlockSpec(memory_space=pltpu.SMEM)] * count


def stay_in_hbm(array):
    return array if INTERPRET else pltpu.with_memory_space_constraint(array, pltpu.HBM)


class Part:
    def __init__(self, array, start=0, size=None):
        self.array, self.start = array, start
        self.shape = (array.shape[0] if size is None else size, *array.shape[1:])
        self.dtype = array.dtype

    def of(self, ref):
        return ref if self.shape == ref.shape else ref.at[pl.ds(self.start, self.shape[0])]


def kernel_call(
    body, out_shape, in_specs, name, moved, loads=(), small=(), carried=(), scratch=()
):
    loads, small, carried = (
        [a if isinstance(a, Part) else Part(a) for a in arrays] for arrays in (loads, small, carried)
    )
    many = isinstance(out_shape, (list, tuple))
    shapes = list(out_shape) if many else [out_shape]
    outs = len(shapes)
    shapes = shapes + [jax.ShapeDtypeStruct(a.shape, a.dtype) for a in carried]
    held = [pltpu.VMEM(a.shape, a.dtype) for a in loads] + [
        pltpu.SMEM(a.shape, a.dtype) for a in small
    ]
    count, more, plain = len(held), len(carried), len(in_specs)

    def run(*refs):
        ins, refs = refs[:plain], refs[plain:]
        sources, refs = refs[: count + more], refs[count + more :]
        results, refs = refs[: outs + more], refs[outs + more :]
        buffers, refs = refs[:count], refs[count:]
        sems, rest = refs[: count + more], refs[count + more :]
        targets = [*buffers, *results[outs:]]
        sources = [a.of(ref) for a, ref in zip((*loads, *small, *carried), sources)]
        moves = [pltpu.make_async_copy(*each) for each in zip(sources, targets, sems)]
        for move in moves:
            move.start()

        def arrive(*which):
            for i in which or range(count):
                moves[i].wait()

        body(arrive, *ins, *buffers, *results[:outs], *rest)
        for move in moves[count:]:
            move.wait()

    call = pl.pallas_call(
        run,
        out_shape=shapes if many or more else shapes[0],
        in_specs=list(in_specs) + [pl.BlockSpec(memory_space=pltpu.HBM)] * (count + more),
        out_specs=in_vmem(outs + more) if many or more else in_vmem(1)[0],
        scratch_shapes=held + [pltpu.SemaphoreType.DMA(())] * (count + more) + list(scratch),
        name=name,
        interpret=INTERPRET,
        compiler_params=pltpu.CompilerParams(vmem_limit_bytes=8 << 20),
        cost_estimate=pl.CostEstimate(flops=300 * moved, bytes_accessed=moved, transcendentals=0),
    )
    return lambda *ins: call(*ins, *[stay_in_hbm(a.array) for a in (*loads, *small, *carried)])


def iota(shape, dim):
    return lax.broadcasted_iota(jnp.int32, shape, dim)


def matmul(a, b):
    return jnp.dot(a, b, preferred_element_type=jnp.float32)


def matmul_t(a, b):
    return lax.dot_general(a, b, (((1,), (1,)), ((), ())), preferred_element_type=jnp.float32)


def scaled_rows(rows, gain):
    mean_sq = jnp.mean(rows * rows, axis=-1, keepdims=True)
    return (rows * lax.rsqrt(mean_sq + EPSILON) * gain).astype(jnp.bfloat16)


def stacked(ref):
    return jnp.concatenate([ref[i].astype(jnp.float32) for i in range(ref.shape[0])], axis=0)


def pack_body(arrive, gate_ref, down_ref, out_ref):
    arrive()
    depth = gate_ref.shape[0]
    units = down_ref.shape[0]
    out_ref[0, :depth] = gate_ref[...]
    for c in range(down_ref.shape[1] // LANES):
        at = depth + units * c
        out_ref[0, at : at + units] = down_ref[:, LANES * c : LANES * (c + 1)]


def join_body(_, first_ref, second_ref, after_ref, out_ref, sem):
    count = first_ref.shape[0]
    move = pltpu.make_async_copy(second_ref, out_ref.at[pl.ds(count, count)], sem)
    move.start()
    out_ref[:count] = first_ref[...]
    move.wait()


def joined(first, second, after, carried=()):
    return kernel_call(
        join_body,
        jax.ShapeDtypeStruct((2 * first.shape[0], *first.shape[1:]), first.dtype),
        in_vmem(1) + [pl.BlockSpec(memory_space=pltpu.HBM), pl.BlockSpec(memory_space=pl.ANY)],
        "join",
        moved=4 << 20,
        carried=carried,
        scratch=[pltpu.SemaphoreType.DMA(())],
    )(first, stay_in_hbm(second), after)


def extend_body(_, first_ref, far_ref, after_ref, out_ref, held_ref, last_ref, sems):
    count = first_ref.shape[0]
    kept = held_ref.shape[0]
    far = [
        pltpu.make_async_copy(far_ref.at[pl.ds(0, kept)], held_ref, sems.at[0]),
        pltpu.make_async_copy(far_ref.at[pl.ds(kept, kept)], last_ref, sems.at[1]),
    ]
    out = [
        pltpu.make_async_copy(first_ref, out_ref.at[pl.ds(0, count)], sems.at[2]),
        pltpu.make_async_copy(held_ref, out_ref.at[pl.ds(count, kept)], sems.at[3]),
        pltpu.make_async_copy(last_ref, out_ref.at[pl.ds(count + kept, kept)], sems.at[4]),
    ]
    for move in (*far, out[0]):
        move.start()
    for i in range(2):
        far[i].wait()
        out[i + 1].start()
    for move in out:
        move.wait()


def extended(first, far, after):
    count, kept = first.shape[0], far.shape[0] // 2
    return pl.pallas_call(
        lambda *refs: extend_body(None, *refs),
        out_shape=[
            jax.ShapeDtypeStruct((2 * count, *first.shape[1:]), first.dtype),
            jax.ShapeDtypeStruct((kept, *first.shape[1:]), first.dtype),
        ],
        in_specs=in_vmem(1)
        + [pl.BlockSpec(memory_space=pltpu.HBM), pl.BlockSpec(memory_space=pl.ANY)],
        out_specs=[pl.BlockSpec(memory_space=pltpu.HBM), *in_vmem(1)],
        scratch_shapes=[
            pltpu.VMEM((kept, *first.shape[1:]), first.dtype),
            pltpu.SemaphoreType.DMA((5,)),
        ],
        name="extend",
        interpret=INTERPRET,
        compiler_params=pltpu.CompilerParams(vmem_limit_bytes=8 << 20),
        cost_estimate=pl.CostEstimate(
            flops=300 * 4 << 20, bytes_accessed=4 << 20, transcendentals=0
        ),
    )(first, stay_in_hbm(far), after)


def project_body(arrive, token_ref, cos_ref, sin_ref, gain_ref, w_ref, q_ref, k_ref, v_ref):
    normed = scaled_rows(stacked(token_ref), gain_ref[...])
    cosine, sine = stacked(cos_ref), stacked(sin_ref)
    first_half = iota(cosine.shape, 1) % HD < HD // 2

    def rotate(part):
        partner = jnp.where(
            first_half,
            pltpu.roll(part, LANES - HD // 2, 1),
            pltpu.roll(part, HD // 2, 1),
        )
        return (part * cosine + partner * sine).astype(jnp.bfloat16)

    queries = rotate(matmul(normed, w_ref[0]))
    for i in range(q_ref.shape[0]):
        q_ref[i] = queries
    k_ref[...] = rotate(matmul(normed, w_ref[1]))
    v_ref[...] = matmul(normed, w_ref[2]).astype(jnp.bfloat16)


def fresh_part(steps, scale, packed, q_ref, k_ref, v_ref, bias_ref, out_ref, lse_ref):
    queries = q_ref[0]
    rows = queries.shape[0]
    packed = jnp.concatenate(
        [jnp.broadcast_to(packed[i : i + 1, :rows], (steps, rows)) for i in range(packed.shape[0])],
        axis=0,
    )
    low_lanes = iota((rows, LANES), 1) < HD
    split = [
        jnp.where(low_lanes, queries, jnp.zeros_like(queries)),
        jnp.where(low_lanes, jnp.zeros_like(queries), queries),
    ]
    row_id, col_id = iota((rows, rows), 0), iota((rows, rows), 1)
    allowed = (row_id // steps == col_id // steps) & (row_id % steps >= col_id % steps)
    same = (packed >> (2 * (row_id % steps))) & 3 == (packed >> (2 * (col_id % steps))) & 3
    outs, lses = [], []
    for head in range(2):
        scores = matmul_t(split[head], k_ref[...]) * scale
        scores = scores + jnp.where(same, bias_ref[0, head], bias_ref[1, head])
        scores = jnp.where(allowed, scores, MASKED_SCORE)
        top = jnp.max(scores, axis=1, keepdims=True)
        weights = jnp.where(allowed, jnp.exp(scores - top), 0.0)
        total = jnp.sum(weights, axis=1, keepdims=True)
        outs.append(matmul(weights.astype(jnp.bfloat16), v_ref[...]) / total)
        lses.append(top + jnp.log(total))
    out_ref[...] = jnp.where(low_lanes, outs[0], outs[1])
    lse_ref[...] = jnp.where(low_lanes, lses[0], lses[1])


def prepare_body(
    steps,
    slots,
    scale,
    arrive,
    seq_ref,
    q_ref,
    k_ref,
    v_ref,
    slot_ref,
    len_ref,
    variate_ref,
    cached_variate_ref,
    bias_ref,
    pick_ref,
    place_ref,
    same_ref,
    bias_mask_ref,
    fresh_ref,
    fresh_lse_ref,
    packed_ref,
):
    requests, pieces = slot_ref.shape
    piece_len = cached_variate_ref.shape[1]
    group = 2 * steps
    rows = slots * group
    arrive()
    table = slot_ref[...]
    packed_row = variate_ref[0:1, :]
    for t in range(1, steps):
        packed_row = packed_row + (variate_ref[t : t + 1, :] << (2 * t))
    columns = jnp.where(iota((8, requests), 0) == 0, packed_row, len_ref[...])
    columns = jnp.transpose(columns.astype(jnp.float32)).astype(jnp.int32)
    packed_variate, length = columns[:, 0:1], columns[:, 1:2]
    packed_ref[...] = jnp.broadcast_to(packed_variate, (requests, LANES))
    own = requests // (requests * steps // q_ref.shape[1])
    packed = packed_ref[pl.ds(pl.multiple_of(seq_ref[0] * own, own), own), :]
    fresh_part(steps, scale, packed, q_ref, k_ref, v_ref, bias_ref, fresh_ref, fresh_lse_ref)

    live = jnp.clip(length - piece_len * iota((requests, pieces), 1), 0, piece_len)
    code = (iota((requests, pieces), 0) << 17) + (packed_variate << 9) + live
    code = code.astype(jnp.float32)
    base = seq_ref[0] * slots
    found = []
    for s in range(slots):
        hit = jnp.where(table == base + s, code, -1.0)
        hit = jnp.max(jnp.max(hit, axis=0, keepdims=True), axis=1, keepdims=True)
        found.append(jnp.broadcast_to(hit, (group, LANES)))
    found = jnp.concatenate(found, axis=0)
    found_lane = jnp.transpose(found)[0:1, :].astype(jnp.int32)
    found = found[:, 0:1].astype(jnp.int32)
    owned = found >= 0
    owner = jnp.where(owned, found >> 17, -1)
    owner_lane = jnp.where(found_lane >= 0, found_lane >> 17, -1)
    row_in = iota((rows, 1), 0) % group
    step_row = row_in % steps
    lane_in = iota((1, rows), 1) % group

    wide = (rows, requests * steps)
    pick_ref[...] = jnp.where(
        iota(wide, 1) == jnp.where(owned, owner * steps + step_row, -1), 1.0, 0.0
    ).astype(jnp.bfloat16)
    tall = (requests * steps, rows)
    place_ref[...] = jnp.where(
        iota(tall, 0) == jnp.where(owner_lane >= 0, owner_lane * steps + lane_in % steps, -1),
        1.0,
        0.0,
    ).astype(jnp.bfloat16)
    same_ref[...] = jnp.where(
        (owner == owner_lane) & (row_in == lane_in), 0.0, FAR
    ).astype(jnp.bfloat16)

    limit = jnp.where(owned, found & 511, 0)
    variate = (found >> (9 + 2 * step_row)) & 3
    first_head = row_in < steps
    same_bias = jnp.where(first_head, bias_ref[0, 0], bias_ref[0, 1])
    other_bias = jnp.where(first_head, bias_ref[1, 0], bias_ref[1, 1])
    cached = jnp.concatenate(
        [
            jnp.broadcast_to(cached_variate_ref[s : s + 1, :], (group, piece_len))
            for s in range(slots)
        ],
        axis=0,
    )
    biases = jnp.where(variate == cached, same_bias, other_bias)
    bias_mask_ref[...] = jnp.where(iota((rows, piece_len), 1) < limit, biases, MASKED_SCORE)


def two_terms(value):
    high = value.astype(jnp.bfloat16)
    return high, (value - high.astype(jnp.float32)).astype(jnp.bfloat16)


def cache_body(
    steps,
    scale,
    arrive,
    q_ref,
    pick_ref,
    place_ref,
    same_ref,
    bias_mask_ref,
    k_ref,
    early_v_ref,
    late_v_ref,
    out_ref,
):
    slots = k_ref.shape[0]
    group = 2 * steps
    rows = slots * group
    devices = out_ref.shape[0]
    span = out_ref.shape[1] // 2
    all_queries = jnp.concatenate([q_ref[i] for i in range(devices)], axis=0)
    picked = matmul(pick_ref[...], all_queries)
    row_head = iota((rows, LANES), 0) % group // steps
    head_match = row_head == iota((rows, LANES), 1) // HD
    picked = jnp.where(head_match, picked, 0.0)
    doubled = jnp.concatenate([picked, picked], axis=1)
    wide = doubled.shape
    own_half = iota(wide, 0) // group % 2 == iota(wide, 1) // LANES
    doubled = jnp.where(own_half, doubled, 0.0).astype(jnp.bfloat16)
    scores = jnp.concatenate(
        [
            matmul_t(
                doubled[group * s : group * (s + 2)],
                jnp.concatenate([k_ref[s], k_ref[s + 1]], axis=1),
            )
            for s in range(0, slots, 2)
        ],
        axis=0,
    )
    bias_mask = bias_mask_ref[...]
    live = bias_mask > 0.5 * MASKED_SCORE
    scores = jnp.where(live, scores * scale + bias_mask, MASKED_SCORE)
    slot_top = jnp.max(scores, axis=1, keepdims=True)
    by_slot = jnp.where(pick_ref[...].astype(jnp.float32) > 0.5, slot_top, MASKED_SCORE)
    tops = by_slot[:group]
    for s in range(1, slots):
        tops = jnp.maximum(tops, by_slot[group * s : group * (s + 1)])
    tops = jnp.where(
        iota(tops.shape, 0) == 0,
        jnp.max(tops[:steps], axis=0, keepdims=True),
        jnp.max(tops[steps:], axis=0, keepdims=True),
    )
    tops = jnp.transpose(tops)
    top_lane = jnp.transpose(jnp.broadcast_to(slot_top, (rows, LANES)))[0:1, :]
    row_top = jnp.max(top_lane + same_ref[...].astype(jnp.float32), axis=1, keepdims=True)
    weights = jnp.where(live, jnp.exp(scores - row_top), 0.0)
    total = jnp.sum(weights, axis=1, keepdims=True)
    arrive()
    values = [r.at[i] for r in (early_v_ref, late_v_ref) for i in range(r.shape[0])]
    weights = weights.astype(jnp.bfloat16)
    mixed = jnp.concatenate(
        [
            matmul(
                weights[group * s : group * (s + 2)],
                jnp.concatenate([values[s][...], values[s + 1][...]], axis=1),
            )
            for s in range(0, slots, 2)
        ],
        axis=0,
    )
    mixed = jnp.where(iota(mixed.shape, 0) // group % 2 == iota(mixed.shape, 1) // LANES, mixed, 0.0)
    mixed = mixed[:, :LANES] + mixed[:, LANES:]
    both = jnp.concatenate(
        [jnp.where(head_match, mixed, 0.0), jnp.where(head_match, total, 0.0)], axis=1
    )
    high, low = two_terms(both)
    place = place_ref[...]
    half = place.shape[0] // 2
    summed = jnp.concatenate(
        [matmul(p, high) + matmul(p, low) for p in (place[:half], place[half:])], axis=0
    )
    out_sum, total_sum = summed[:, :LANES], summed[:, LANES:]
    low_lanes = iota(out_sum.shape, 1) < HD
    top = jnp.where(low_lanes, tops[:, 0:1], tops[:, 1:2])
    some = total_sum > 0.0
    safe_total = jnp.where(some, total_sum, 1.0)
    averaged = jnp.where(some, out_sum / safe_total, 0.0).astype(jnp.bfloat16)
    lse = jnp.where(some, top + jnp.log(safe_total), MASKED_SCORE)
    lse_high = lse.astype(jnp.bfloat16).astype(jnp.float32)
    rest = lse - lse_high
    lse_mid = rest.astype(jnp.bfloat16).astype(jnp.float32)
    place_in = iota(out_sum.shape, 1) % HD
    coded = jnp.where(
        place_in == 0,
        lse_high,
        jnp.where(place_in == 1, lse_mid, jnp.where(place_in == 2, rest - lse_mid, 0.0)),
    ).astype(jnp.bfloat16)
    for d in range(devices):
        out_ref[d, :span] = averaged[span * d : span * (d + 1)]
        out_ref[d, span:] = coded[span * d : span * (d + 1)]


def finish_body(arrive, part_ref, fresh_ref, fresh_lse_ref, w_ref, out_ref):
    devices = part_ref.shape[0]
    span = part_ref.shape[1] // 2
    source, lane = iota((LANES, LANES), 0), iota((LANES, LANES), 1)
    decode = jnp.where((source // HD == lane // HD) & (source % HD < 3), 1.0, 0.0)
    decode = decode.astype(jnp.bfloat16)
    lses = [matmul(part_ref[d, span:], decode) for d in range(devices)]
    top = fresh_lse_ref[...]
    for lse in lses:
        top = jnp.maximum(top, lse)
    weight = jnp.exp(fresh_lse_ref[...] - top)
    total = weight
    mixed = weight * fresh_ref[...]
    for d in range(devices):
        weight = jnp.exp(lses[d] - top)
        total = total + weight
        mixed = mixed + weight * part_ref[d, :span].astype(jnp.float32)
    attended = (mixed / total).astype(jnp.bfloat16)
    partial = matmul(attended, w_ref[...]).astype(jnp.bfloat16)
    for d in range(out_ref.shape[0]):
        out_ref[d] = partial


def gated(normed, blocks):
    low_lanes = iota((normed.shape[0], LANES), 1) < HD
    pair = jnp.concatenate([block[: normed.shape[1]] for block in blocks], axis=1)
    expanded = matmul(normed, pair)
    gates = expanded / (1.0 + jnp.exp(-expanded))
    first = gates[:, :LANES] * pltpu.roll(expanded[:, :LANES], HD, 1)
    second = pltpu.roll(gates[:, LANES:], HD, 1) * expanded[:, LANES:]
    return jnp.where(low_lanes, first, second)


def settle_body(_, part_ref, token_ref, gain_ref, normed_ref, mid_ref):
    mid = part_ref[0].astype(jnp.float32)
    for d in range(1, part_ref.shape[0]):
        mid = mid + part_ref[d].astype(jnp.float32)
    mid = mid + stacked(token_ref)
    own = mid_ref.shape[1]
    for d in range(mid_ref.shape[0]):
        mid_ref[d] = mid[own * d : own * (d + 1)]
    normed_ref[...] = scaled_rows(mid, gain_ref[...])


def feed_body(_, normed_ref, own_w_ref, near_w_ref, held_w_ref, far_ref, out_ref, last_w_ref, sem):
    move = pltpu.make_async_copy(
        far_ref.at[pl.ds(held_w_ref.shape[0], last_w_ref.shape[0])], last_w_ref, sem
    )
    move.start()
    own = out_ref.shape[1]
    normed = normed_ref[...]
    width = normed.shape[1]
    refs = (own_w_ref, near_w_ref, held_w_ref, last_w_ref)
    blocks = [r.at[i] for r in refs for i in range(r.shape[0])]
    halves = []
    for s in range(0, len(blocks), 2):
        if s + 2 == len(blocks):
            move.wait()
        halves.append(gated(normed, blocks[s : s + 2]))
    hidden = jnp.concatenate(halves, axis=1).astype(jnp.bfloat16)
    for c in range(0, width // LANES, 2):
        at = width + HD * c
        weights = jnp.concatenate(
            [
                jnp.concatenate([block[at : at + HD], block[at + HD : at + 2 * HD]], axis=1)
                for block in blocks
            ],
            axis=0,
        )
        part = matmul(hidden, weights).astype(jnp.bfloat16)
        for d in range(out_ref.shape[0]):
            out_ref[d, :, LANES * c : LANES * (c + 2)] = part[own * d : own * (d + 1)]


def last_body(arrive, index_ref, part_ref, mid_ref, out_ref):
    total = mid_ref[index_ref[0]]
    summed = part_ref[0].astype(jnp.float32)
    for d in range(1, part_ref.shape[0]):
        summed = summed + part_ref[d].astype(jnp.float32)
    out_ref[...] = (total + summed).astype(jnp.bfloat16)


def rotation_tables(lengths, steps):
    half = HD // 2
    lane = np.arange(LANES)
    inv_freq = (10000.0 ** (-(lane % half) / half)).astype(np.float32)
    sign = np.where(lane % HD < half, -1.0, 1.0).astype(np.float32)
    offsets = jnp.arange(steps, dtype=jnp.int32)
    positions = (lengths[:, None, None] + offsets[None, :, None]).astype(jnp.float32)
    angles = positions * inv_freq
    return jnp.cos(angles), jnp.sin(angles) * sign


def on_device(
    tokens,
    w_qkv,
    w_out,
    variate_bias,
    attn_gain,
    ffn_gain,
    gate_up,
    w_down,
    cache_keys,
    cache_values,
    cache_variate,
    new_variate,
    piece_slot,
    cache_len,
):
    row_count, width = tokens.shape
    requests, steps = new_variate.shape
    slots, piece_len, lanes = cache_keys.shape
    seqs, tps = lax.axis_size("seq"), lax.axis_size("tp")
    rows = row_count * tps
    own_requests = rows // steps
    scale = 1.0 / math.sqrt(HD)
    bf16, f32 = jnp.bfloat16, jnp.float32
    shape = jax.ShapeDtypeStruct
    seq_at = lax.axis_index("seq")
    tp_at = lax.axis_index("tp").astype(jnp.int32).reshape(1)

    row_tokens = exchange(jnp.broadcast_to(tokens[None], (tps, *tokens.shape)), "tp")

    blocks, units = w_down.shape[:2]
    ffn_weights, qkv_weights, qkv_gain = kernel_call(
        pack_body,
        shape((1, width + units * width // lanes, lanes), bf16),
        [],
        "pack",
        moved=1 << 20,
        loads=[gate_up.reshape(width, lanes), w_down.reshape(units, width)],
        carried=[w_qkv.transpose(1, 0, 2), attn_gain[None, :]],
    )()
    ffn_next = swapped(ffn_weights, [2, 7, 0, 5, 6, 3, 4, 1])

    own_len = lax.dynamic_slice_in_dim(cache_len, seq_at * own_requests, own_requests, 0)
    cosine, sine = rotation_tables(own_len, steps)
    queries, keys_new, values_new = kernel_call(
        project_body,
        [shape((seqs, rows, lanes), bf16), shape((rows, lanes), bf16), shape((rows, lanes), bf16)],
        in_vmem(5),
        "project",
        moved=1 << 20,
    )(row_tokens, cosine, sine, qkv_gain, qkv_weights)
    all_queries = exchange(queries, "seq")

    slot_rows = 2 * steps * slots
    early = slots // 2
    pick, place, same, bias_mask, fresh, fresh_lse, held_values = kernel_call(
        lambda *refs: prepare_body(steps, slots, scale, *refs),
        [
            shape((slot_rows, requests * steps), bf16),
            shape((requests * steps, slot_rows), bf16),
            shape((slot_rows, slot_rows), bf16),
            shape((slot_rows, piece_len), f32),
            shape((rows, lanes), f32),
            shape((rows, lanes), f32),
        ],
        in_smem(1) + in_vmem(3),
        "prepare",
        moved=1 << 20,
        loads=[piece_slot, cache_len[None, :], new_variate.T, cache_variate],
        small=[variate_bias],
        carried=[Part(cache_values, 0, early)],
        scratch=[pltpu.VMEM((requests, lanes), jnp.int32)],
    )(seq_at.astype(jnp.int32).reshape(1), queries, keys_new, values_new)

    partial = kernel_call(
        lambda *refs: cache_body(steps, scale, *refs),
        shape((seqs, 2 * rows, lanes), bf16),
        in_vmem(7),
        "cache",
        moved=4 << 20,
        loads=[Part(cache_values, early, slots - early)],
    )(all_queries, pick, place, same, bias_mask, cache_keys, held_values)
    ffn_weights, out_weights, gain = joined(
        ffn_weights, ffn_next, partial, [w_out, ffn_gain[None, :]]
    )
    partial = exchange(partial, "seq")

    ffn_far = swapped(ffn_weights, [6, 3, 4, 1, 2, 7, 0, 5])
    mid_parts = kernel_call(
        finish_body,
        shape((tps, rows, width), bf16),
        in_vmem(4),
        "finish",
        moved=30 << 20,
    )(partial, fresh, fresh_lse, out_weights)
    ffn_all, ffn_held = extended(ffn_weights, ffn_far, mid_parts)
    mid_parts = exchange(mid_parts, "tp")
    ffn_near = swapped(ffn_all, [1, 0, 3, 2, 5, 4, 7, 6])
    normed, mid = kernel_call(
        settle_body,
        [shape((rows, width), bf16), shape((tps, row_count, width), f32)],
        in_vmem(3),
        "settle",
        moved=30 << 20,
    )(mid_parts, row_tokens, gain)
    ffn_parts = kernel_call(
        feed_body,
        shape((tps, row_count, width), bf16),
        in_vmem(4) + [pl.BlockSpec(memory_space=pltpu.HBM)],
        "feed",
        moved=4 << 20,
        scratch=[pltpu.VMEM(ffn_held.shape, bf16), pltpu.SemaphoreType.DMA(())],
    )(normed, ffn_weights, ffn_near, ffn_held, stay_in_hbm(ffn_far))
    ffn_parts = exchange(ffn_parts, "tp")
    return kernel_call(
        last_body, shape((row_count, width), bf16), in_smem(1) + in_vmem(2), "last", moved=1 << 17
    )(tp_at, ffn_parts, mid)


def solution(mesh):
    in_specs = (
        P(("req", "seq", "tp"), None),
        P(None, None, "tp"),
        P("tp", None),
        P(None, "tp"),
        P(),
        P(),
        P(None, ("seq", "tp"), None),
        P(("seq", "tp"), None, None),
        P(("req", "seq"), None, "tp"),
        P(("req", "seq"), None, "tp"),
        P(("req", "seq"), None),
        P("req", None),
        P("req", None),
        P("req"),
    )
    out_specs = P(("req", "seq", "tp"), None)
    return jax.shard_map(
        on_device, mesh=mesh, in_specs=in_specs, out_specs=out_specs, check_vma=False
    )
```
